128 devices in a mesh: node: 8 (over z, core), event: 16 (over x, y).
Axes of the slice: x: 4, y: 4, z: 4, core: 2. Of those that a mesh axis runs over, the one named last changes fastest.
Arguments:
- memory: bfloat16 [16384, 256], P('node'), may hold values from -6 to 6
- event_feat: bfloat16 [128, 128, 16, 128], P(('node', 'event')), may hold values from -6 to 6
- event_source: int32 [128, 128, 16], P(('node', 'event')), may hold values from 0 to 2047
- event_partner: int32 [128, 128, 16], P(('node', 'event')), may hold values from 0 to 1023
- event_negative: int32 [128, 128, 16], P(('node', 'event')), may hold values from 0 to 1023
- event_time: int32 [128, 128, 16], P(('node', 'event')), may hold values from 0 to 1023
- event_count: int32 [128, 128], P(('node', 'event')), may hold values from 0 to 16, as said below
- requests: int32 [128, 8, 128], P(('node', 'event')), may hold values from 0 to 2047
- w_input: bfloat16 [512, 768], replicated, may hold values from -0.25 to 0.25
- w_state: bfloat16 [256, 768], replicated, may hold values from -0.375 to 0.375
- w_pair: bfloat16 [256, 256], replicated, may hold values from -0.375 to 0.375
- gate_bias: float32 [768], replicated, may hold values from -3 to 3
- time_freq: float32 [128], replicated, may hold values from 0.001 to 1
Outputs:
- memory_grad: float32 [16384, 256], P(('node', 'event'))
The draws below stay inside these ranges and needn't reach their ends.
Inputs may be any that keep to these rules, and one draw needn't show every extreme that they name: `event_count`: in every draw some device receives 16 live slots from every time block.
All inputs are finite; a program needn't handle non-finite values.
Results may differ from the reference program's by a relative error of at most 0.0021.
Values may be sent and summed in bfloat16 or wider, within the bound.
No kernel may reach another device: no remote copies, remote signals or barrier semaphores. Data moves between devices by JAX's collectives and lax.ppermute only.
A program may use at most 64 MiB of HBM per device.

```python
import math
import jax
import jax.numpy as jnp
from jax import lax

DM = 256
EF = 128
TE = 128
TBINS = 1024
CAP = 16
PCAP = 128
NODE_GRP = 2048
SHARDS = 128
NODES = 16384
TABLE = 1024
DIN = 512
N_NODE = 8
N_EVENT = 16


def draw_event_count(key, part):
    first = jax.random.fold_in(key, 11)
    second = jax.random.fold_in(key, 12)
    third = jax.random.fold_in(key, 13)
    base = jax.random.randint(first, (SHARDS, SHARDS), 0, CAP + 1)
    weight = jax.random.randint(second, (1, SHARDS), 1, 5)
    counts = jnp.minimum(CAP, base * weight // 2)
    full = jax.random.randint(third, (), 0, SHARDS)
    column = jnp.arange(SHARDS, dtype=jnp.int32)[None, :] == full
    return jnp.where(column, CAP, counts).astype(jnp.int32)


def with_ends(array, stream_key, least, top_value):
    extent = array.shape
    place = [jax.random.randint(jax.random.fold_in(stream_key, axis), (), 0, extent[axis]) for axis in range(len(extent))]
    array = array.at[tuple(place)].set(least)
    longest = extent.index(max(extent))
    place[longest] = (place[longest] + 1) % extent[longest]
    return array.at[tuple(place)].set(top_value)


def level_of(key, shape, shards, least, largest):
    gain, own = 1.0, jax.random.fold_in(key, 6)
    for axis_at, blocks in shards:
        heights = jnp.exp(jax.random.uniform(jax.random.fold_in(own, axis_at), (blocks,), jnp.float32, least / len(shards), largest / len(shards)))
        gain = gain * jnp.repeat(heights, shape[axis_at] // blocks).reshape([-1 if axis == axis_at else 1 for axis in range(len(shape))])
    return gain


def gaussian(own_key, dims, scale, bound, pieces=(), held_as=jnp.bfloat16):
    drawn = scale * jax.random.normal(own_key, dims, jnp.float32)
    if pieces:
        drawn = drawn * level_of(own_key, dims, pieces, -0.22, 0.18)
    return jnp.clip(drawn, -bound, bound).astype(held_as)


def setup_inputs(seed: int = 0) -> dict:
    seeds = jax.random.split(jax.random.key(seed), 14)
    memory = gaussian(seeds[0], (NODES, DM), 1.0, 6.0, ((0, 8),))
    event_feat = gaussian(seeds[1], (SHARDS, SHARDS, CAP, EF), 1.0, 6.0, ((0, 128),))
    event_source = with_ends(jax.random.randint(seeds[2], (SHARDS, SHARDS, CAP), 0, NODE_GRP), jax.random.fold_in(seeds[2], 1), 0, NODE_GRP - 1).astype(jnp.int32)
    event_partner = with_ends(jax.random.randint(seeds[3], (SHARDS, SHARDS, CAP), 0, TABLE), jax.random.fold_in(seeds[3], 1), 0, TABLE - 1).astype(jnp.int32)
    event_negative = with_ends(jax.random.randint(seeds[4], (SHARDS, SHARDS, CAP), 0, TABLE), jax.random.fold_in(seeds[4], 1), 0, TABLE - 1).astype(jnp.int32)
    event_time = with_ends(jax.random.randint(seeds[5], (SHARDS, SHARDS, CAP), 0, TBINS), jax.random.fold_in(seeds[5], 1), 0, TBINS - 1).astype(jnp.int32)
    event_count = draw_event_count(jax.random.fold_in(seeds[13], 71), 0)
    requests = with_ends(jax.random.randint(seeds[7], (SHARDS, N_NODE, PCAP), 0, NODE_GRP), jax.random.fold_in(seeds[7], 1), 0, NODE_GRP - 1).astype(jnp.int32)
    w_input = gaussian(seeds[8], (DIN, 3 * DM), DIN ** -0.5, 0.25)
    w_state = gaussian(seeds[9], (DM, 3 * DM), DM ** -0.5, 0.375)
    w_pair = gaussian(seeds[10], (DM, DM), DM ** -0.5, 0.375)
    gate_bias = gaussian(seeds[11], (3 * DM,), 0.5, 3.0, (), jnp.float32)
    time_freq = jnp.clip(jnp.exp(jax.random.uniform(seeds[12], (TE,), jnp.float32, math.log(0.001), math.log(1.0))), 0.001, 1.0)
    return {"memory": memory, "event_feat": event_feat, "event_source": event_source, "event_partner": event_partner, "event_negative": event_negative, "event_time": event_time, "event_count": event_count, "requests": requests, "w_input": w_input, "w_state": w_state, "w_pair": w_pair, "gate_bias": gate_bias, "time_freq": time_freq}


def pair_grads(current, partner, negative, feature, timing, valid, w_input, w_state, w_pair, gate_bias):
    width = current.shape[1]
    joined = jnp.concatenate([partner, feature, timing], axis=1)
    from_input = jnp.dot(joined, w_input, preferred_element_type=jnp.float32)
    from_state = jnp.dot(current, w_state, preferred_element_type=jnp.float32)
    reset = jax.nn.sigmoid(from_input[:, :width] + from_state[:, :width] + gate_bias[:width])
    update = jax.nn.sigmoid(from_input[:, width:2 * width] + from_state[:, width:2 * width] + gate_bias[width:2 * width])
    recurrent = from_state[:, 2 * width:]
    candidate = jnp.tanh(from_input[:, 2 * width:] + gate_bias[2 * width:] + reset * recurrent)
    previous = current.astype(jnp.float32)
    renewed = (1.0 - update) * candidate + update * previous
    factor = 1.0 / math.sqrt(width)
    key_pos = jnp.dot(partner, w_pair, preferred_element_type=jnp.float32)
    key_neg = jnp.dot(negative, w_pair, preferred_element_type=jnp.float32)
    score_pos = lax.optimization_barrier(jnp.sum(renewed * key_pos, axis=1)) * factor
    score_neg = lax.optimization_barrier(jnp.sum(renewed * key_neg, axis=1)) * factor
    weight_pos = -valid * jax.nn.sigmoid(-score_pos)
    weight_neg = valid * jax.nn.sigmoid(score_neg)
    grad_renewed = (weight_pos[:, None] * key_pos + weight_neg[:, None] * key_neg) * factor
    grad_keypos = (weight_pos[:, None] * renewed * factor).astype(jnp.bfloat16)
    grad_keyneg = (weight_neg[:, None] * renewed * factor).astype(jnp.bfloat16)
    grad_cand = grad_renewed * (1.0 - update) * (1.0 - candidate * candidate)
    grad_reset = grad_cand * recurrent * reset * (1.0 - reset)
    grad_update = grad_renewed * (previous - candidate) * update * (1.0 - update)
    input_back = jnp.concatenate([grad_reset, grad_update, grad_cand], axis=1).astype(jnp.bfloat16)
    state_back = jnp.concatenate([grad_reset, grad_update, grad_cand * reset], axis=1).astype(jnp.bfloat16)
    through_input = jnp.dot(input_back, w_input.T, preferred_element_type=jnp.float32)
    grad_current = grad_renewed * update + jnp.dot(state_back, w_state.T, preferred_element_type=jnp.float32)
    grad_partner = through_input[:, :width] + jnp.dot(grad_keypos, w_pair.T, preferred_element_type=jnp.float32)
    grad_negative = jnp.dot(grad_keyneg, w_pair.T, preferred_element_type=jnp.float32)
    return (grad_current, grad_partner, grad_negative)

def reference(memory, event_feat, event_source, event_partner, event_negative, event_time, event_count, requests, w_input, w_state, w_pair, gate_bias, time_freq):
    slots = SHARDS * CAP
    owners = jnp.arange(N_NODE, dtype=jnp.int32)[:, None] * NODE_GRP
    table_ids = (owners[None, :, :] + requests).reshape(SHARDS, N_NODE * PCAP)
    column = jnp.arange(CAP, dtype=jnp.int32)

    def one_device(total, target):
        feature = event_feat[:, target].reshape(slots, EF)
        group = target // N_EVENT
        source_ids = group * NODE_GRP + event_source[:, target].reshape(slots)
        listed = table_ids[target]
        partner_ids = listed[event_partner[:, target].reshape(slots)]
        negative_ids = listed[event_negative[:, target].reshape(slots)]
        timing = jnp.cos(event_time[:, target].reshape(slots).astype(jnp.float32)[:, None] * time_freq[None, :]).astype(jnp.bfloat16)
        valid = (column[None, :] < event_count[:, target][:, None]).astype(jnp.float32).reshape(slots)
        grad_current, grad_partner, grad_negative = pair_grads(memory[source_ids], memory[partner_ids], memory[negative_ids], feature, timing, valid, w_input, w_state, w_pair, gate_bias)
        total = total.at[source_ids].add(grad_current)
        total = total.at[partner_ids].add(grad_partner)
        total = total.at[negative_ids].add(grad_negative)
        return (total, None)
    total, _ = lax.scan(one_device, jnp.zeros((NODES, DM), jnp.float32), jnp.arange(SHARDS, dtype=jnp.int32))
    return total
```

```python
import functools

import jax
import jax.numpy as jnp
from jax import lax
from jax.experimental import pallas as pl
from jax.experimental.pallas import tpu as pltpu
from jax.sharding import PartitionSpec as P

F32 = jnp.float32
BF16 = jnp.bfloat16


def dot(a, b):
    return jnp.dot(a, b, preferred_element_type=F32)


def dot_nt(a, b):
    return lax.dot_general(a, b, (((1,), (1,)), ((), ())), preferred_element_type=F32)


def iota(shape, dim):
    return lax.broadcasted_iota(jnp.int32, shape, dim)


def split(x):
    high = x.astype(BF16)
    low = (x - high.astype(F32)).astype(BF16)
    return high, low


def call(kernel, outs, args, grid=None, in_specs=None, out_specs=None, scratch=(), flops=0, moved=0, trans=0, name=None, prefetch=0):
    spec = pltpu.PrefetchScalarGridSpec(
        num_scalar_prefetch=prefetch,
        grid=grid or (1,),
        in_specs=in_specs,
        out_specs=out_specs,
        scratch_shapes=list(scratch),
    )
    return pl.pallas_call(
        kernel,
        out_shape=outs,
        grid_spec=spec,
        name=name,
        compiler_params=pltpu.CompilerParams(vmem_limit_bytes=48 << 20),
        cost_estimate=pl.CostEstimate(flops=int(flops), bytes_accessed=int(moved), transcendentals=int(trans)),
    )(*args)


def whole(shape):
    return pl.BlockSpec(shape, lambda *_: (0,) * len(shape))


def pack_kernel(group_rows, table_rows, feat, source, partner, negative, time, count, wanted, out):
    shards, slots, width = feat.shape
    groups = wanted.shape[0]
    live = iota((slots, shards), 0) < count[...]
    fields = (
        jnp.where(live, source[...], group_rows),
        jnp.where(live, partner[...], table_rows),
        jnp.where(live, negative[...], table_rows),
        time[...],
    )
    parts = []
    for field in fields:
        parts += [(field >> 8).astype(F32), (field & 255).astype(F32)]
    ids = jnp.concatenate(parts, axis=0).T
    rows = (shards, 8, width)

    def spread(x):
        return jnp.broadcast_to(x[:, None, :], rows)

    def by_group(x):
        return jnp.broadcast_to(x[:, None, :], (groups, shards // groups, width)).reshape(shards, width)

    place = iota(rows, 1)
    high = by_group((wanted[...] >> 8).astype(F32))
    low = by_group((wanted[...] & 255).astype(F32))
    tail = jnp.where(place == 0, spread(ids), jnp.where(place == 1, spread(high), spread(low)))
    out[:, 0:slots, :] = feat[...]
    out[:, slots : slots + 8, :] = tail.astype(BF16)


def field_columns(tail, field):
    blocks = tail.shape[0]
    row = tail[...].astype(F32)[:, 0:1, :]
    spread = jnp.broadcast_to(row, (blocks, 16, 128)).reshape(blocks * 16, 128)
    shape = (blocks * 16, 128)
    masked = jnp.where((iota(shape, 1) & 15) == (iota(shape, 0) & 15), spread, 0.0).astype(BF16)
    lane = iota((128, 128), 0) >> 4
    weight = jnp.where(lane == 2 * field, 256.0, jnp.where(lane == 2 * field + 1, 1.0, 0.0)).astype(BF16)
    return masked, weight


def columns_of(masked, weight):
    return dot(masked, weight)


def rows_of(masked, weight):
    return dot_nt(weight.T[0:8, :], masked)


def one_hot_columns(values, count):
    rows = values.shape[0]
    ids = values.astype(jnp.int32)
    pieces = [
        jnp.where(iota((rows, 128), 1) == ids - 128 * t, 1.0, 0.0).astype(BF16) for t in range(count // 128)
    ]
    return jnp.concatenate(pieces, axis=1)


def one_hot_rows(values, count, start=0):
    shape = (count, values.shape[1])
    ids = jnp.broadcast_to(values.astype(jnp.int32) - start, shape)
    return jnp.where(iota(shape, 0) == ids, 1.0, 0.0).astype(BF16)


def wanted_values(tail):
    rows = tail[...].astype(F32)[:, 0]
    return rows[:, 1], rows[:, 2]


def fetch_kernel(place, tail, memory, out):
    high, low = wanted_values(tail)
    groups = high.shape[0]
    shape = (groups * 128, 128)
    here = iota(shape, 1) == (iota(shape, 0) & 127)

    def spread(x):
        wide = jnp.broadcast_to(x[:, None, :], (groups, 128, 128)).reshape(shape)
        return jnp.where(here, wide, 0.0).astype(BF16)

    joined = jnp.concatenate([spread(high), spread(low)], axis=1)
    weight = jnp.where(iota((256, 128), 0) < 128, 256.0, 1.0).astype(BF16)
    values = dot(joined, weight)
    selector = one_hot_columns(values, memory.shape[0])
    out[...] = dot(selector, memory[...]).astype(BF16)


def source_kernel(tail, memory, freq, current, timing, rows):
    masked, weight = field_columns(tail, 0)
    values = columns_of(masked, weight)
    rows[...] = rows_of(masked, weight)
    selector = one_hot_columns(values, memory.shape[0])
    current[...] = dot(selector, memory[...]).astype(BF16)
    _, weight = field_columns(tail, 3)
    timing[...] = jnp.cos(columns_of(masked, weight) * freq[...]).astype(BF16)


def step_kernel(message, table, current_ref, timing, w_input, w_state, w_pair, bias, table_grad, grad_high, grad_low, acc, acc_neg):
    at = pl.program_id(0)
    table_rows, width = table.shape
    blocks = message.shape[0]
    events = blocks * 16
    feature = message[:, 0:16, :].reshape(events, 128)
    tail = message[:, 16:24, :]
    masked, weight_p = field_columns(tail, 1)
    _, weight_n = field_columns(tail, 2)
    partner = dot(one_hot_columns(columns_of(masked, weight_p), table_rows), table[...]).astype(BF16)
    negative = dot(one_hot_columns(columns_of(masked, weight_n), table_rows), table[...]).astype(BF16)
    current = current_ref[...]
    joined = jnp.concatenate([partner, feature, timing[...]], axis=1)
    w_in = w_input[...]
    from_input = dot(joined, w_in)
    from_state = dot(current, w_state[...])
    gate = bias[...]
    reset = jax.nn.sigmoid(from_input[:, :width] + from_state[:, :width] + gate[:, :width])
    update = jax.nn.sigmoid(
        from_input[:, width : 2 * width] + from_state[:, width : 2 * width] + gate[:, width : 2 * width]
    )
    recurrent = from_state[:, 2 * width :]
    candidate = jnp.tanh(from_input[:, 2 * width :] + gate[:, 2 * width :] + reset * recurrent)
    previous = current.astype(F32)
    renewed = (1.0 - update) * candidate + update * previous
    factor = 1.0 / width**0.5
    key_pos = dot(partner, w_pair[...])
    key_neg = dot(negative, w_pair[...])
    score_pos = jnp.sum(renewed * key_pos, axis=1, keepdims=True) * factor
    score_neg = jnp.sum(renewed * key_neg, axis=1, keepdims=True) * factor
    weight_pos = -jax.nn.sigmoid(-score_pos)
    weight_neg = jax.nn.sigmoid(score_neg)
    grad_renewed = (weight_pos * key_pos + weight_neg * key_neg) * factor
    grad_keypos = (weight_pos * renewed * factor).astype(BF16)
    grad_keyneg = (weight_neg * renewed * factor).astype(BF16)
    grad_cand = grad_renewed * (1.0 - update) * (1.0 - candidate * candidate)
    grad_reset = grad_cand * recurrent * reset * (1.0 - reset)
    grad_update = grad_renewed * (previous - candidate) * update * (1.0 - update)
    first = grad_reset.astype(BF16)
    second = grad_update.astype(BF16)
    input_back = jnp.concatenate([first, second, grad_cand.astype(BF16)], axis=1)
    state_back = jnp.concatenate([first, second, (grad_cand * reset).astype(BF16)], axis=1)
    grad_current = grad_renewed * update + dot_nt(state_back, w_state[...])
    high, low = split(grad_current)
    grad_high[...] = high
    grad_low[...] = low
    grad_partner = dot_nt(input_back, w_in[:width, :]) + dot_nt(grad_keypos, w_pair[...])
    high, low = split(grad_partner)
    to_partner = one_hot_rows(rows_of(masked, weight_p)[0:1, :], table_rows)
    to_negative = one_hot_rows(rows_of(masked, weight_n)[0:1, :], table_rows)
    added = dot(to_partner, high) + dot(to_partner, low)
    added_neg = dot(to_negative, grad_keyneg)

    @pl.when(at == 0)
    def _():
        acc[...] = added
        acc_neg[...] = added_neg

    @pl.when(at > 0)
    def _():
        acc[...] += added
        acc_neg[...] += added_neg

    @pl.when(at == pl.num_programs(0) - 1)
    def _():
        high, low = split(acc_neg[...])
        total = acc[...] + dot_nt(high, w_pair[...]) + dot_nt(low, w_pair[...])
        table_grad[...] = total.astype(BF16)


def source_scatter_kernel(rows, grad_high, grad_low, out):
    count = out.shape[0]
    selector = one_hot_rows(rows[0:1, :], count, pl.program_id(0) * count)
    out[...] = dot(selector, grad_high[...]) + dot(selector, grad_low[...])


def returned_kernel(place, tail, returned, state_grad, out):
    high, low = wanted_values(tail)
    values = high * 256.0 + low
    count = out.shape[0]
    start = pl.program_id(0) * count
    pieces = [one_hot_rows(values[g : g + 1, :], count, start) for g in range(values.shape[0])]
    selector = jnp.concatenate(pieces, axis=1)
    out[...] = (state_grad[...] + dot(selector, returned[...])).astype(BF16)


def local(
    memory,
    event_feat,
    event_source,
    event_partner,
    event_negative,
    event_time,
    event_count,
    requests,
    w_input,
    w_state,
    w_pair,
    gate_bias,
    time_freq,
):
    nodes = lax.axis_size("node")
    peers = lax.axis_size("event")
    shards = nodes * peers
    group_rows, width = memory.shape
    _, groups, per_group = requests.shape
    table_rows = groups * per_group
    slots, feat_width = event_feat.shape[2:]
    events = shards * slots

    flat = [x[0].T for x in (event_source, event_partner, event_negative, event_time)]
    args = (event_feat[0], *flat, event_count, requests[0])
    message = call(
        functools.partial(pack_kernel, group_rows, table_rows),
        jax.ShapeDtypeStruct((shards, slots + 8, feat_width), BF16),
        args,
        in_specs=[whole(x.shape) for x in args],
        out_specs=whole((shards, slots + 8, feat_width)),
        moved=2 * events * feat_width * 2,
        name="pack",
    )
    message = lax.all_to_all(message, ("node", "event"), 0, 0, tiled=True)
    place = lax.axis_index("event").astype(jnp.int32).reshape(1)
    by_peer = message.reshape(nodes, peers, slots + 8, feat_width)
    tail_spec = pl.BlockSpec((nodes, 1, 8, feat_width), lambda i, at: (0, at[0], slots // 8, 0))
    fetched = call(
        fetch_kernel,
        jax.ShapeDtypeStruct((table_rows, width), BF16),
        (place, by_peer, memory),
        in_specs=[tail_spec, whole(memory.shape)],
        out_specs=whole((table_rows, width)),
        flops=2 * table_rows * group_rows * width,
        moved=group_rows * width * 2,
        name="fetch",
        prefetch=1,
    )
    table = lax.all_to_all(fetched.reshape(groups, per_group, width), "node", 0, 0, tiled=True).reshape(table_rows, width)

    block = 512
    turns = events // block
    rows_block = lambda i: (i, 0)
    current, timing, rows = call(
        source_kernel,
        (
            jax.ShapeDtypeStruct((events, width), BF16),
            jax.ShapeDtypeStruct((events, feat_width), BF16),
            jax.ShapeDtypeStruct((8, events), F32),
        ),
        (message, memory, time_freq.reshape(1, -1)),
        grid=(turns,),
        in_specs=[
            pl.BlockSpec((block // slots, 8, feat_width), lambda i: (i, slots // 8, 0)),
            whole(memory.shape),
            whole((1, feat_width)),
        ],
        out_specs=(
            pl.BlockSpec((block, width), rows_block),
            pl.BlockSpec((block, feat_width), rows_block),
            pl.BlockSpec((8, block), lambda i: (0, i)),
        ),
        flops=2 * events * group_rows * width,
        moved=4 * events * width,
        trans=events * feat_width,
        name="source",
    )
    table_grad, grad_high, grad_low = call(
        step_kernel,
        (
            jax.ShapeDtypeStruct((table_rows, width), BF16),
            jax.ShapeDtypeStruct((events, width), BF16),
            jax.ShapeDtypeStruct((events, width), BF16),
        ),
        (message, table, current, timing, w_input, w_state, w_pair, gate_bias.reshape(1, -1)),
        grid=(turns,),
        in_specs=[
            pl.BlockSpec((block // slots, slots + 8, feat_width), lambda i: (i, 0, 0)),
            whole(table.shape),
            pl.BlockSpec((block, width), rows_block),
            pl.BlockSpec((block, feat_width), rows_block),
            whole(w_input.shape),
            whole(w_state.shape),
            whole(w_pair.shape),
            whole((1, 3 * width)),
        ],
        out_specs=(
            whole((table_rows, width)),
            pl.BlockSpec((block, width), rows_block),
            pl.BlockSpec((block, width), rows_block),
        ),
        scratch=[pltpu.VMEM((table_rows, width), F32), pltpu.VMEM((table_rows, width), F32)],
        flops=2 * events * width * (5 * table_rows + 3 * 4 * width + 3 * 3 * width),
        moved=8 * events * width,
        trans=events * width * 3,
        name="step",
    )
    returned = lax.all_to_all(table_grad.reshape(groups, per_group, width), "node", 0, 0, tiled=True).reshape(table_rows, width)
    node_block = 512
    state_grad = call(
        source_scatter_kernel,
        jax.ShapeDtypeStruct((group_rows, width), F32),
        (rows, grad_high, grad_low),
        grid=(group_rows // node_block,),
        in_specs=[whole(rows.shape), whole(grad_high.shape), whole(grad_low.shape)],
        out_specs=pl.BlockSpec((node_block, width), rows_block),
        flops=4 * events * group_rows * width,
        moved=8 * events * width,
        name="scatter",
    )
    total = call(
        returned_kernel,
        jax.ShapeDtypeStruct((group_rows, width), BF16),
        (place, by_peer, returned, state_grad),
        grid=(group_rows // node_block,),
        in_specs=[
            tail_spec,
            pl.BlockSpec((table_rows, width), lambda i, at: (0, 0)),
            pl.BlockSpec((node_block, width), lambda i, at: (i, 0)),
        ],
        out_specs=pl.BlockSpec((node_block, width), lambda i, at: (i, 0)),
        flops=2 * table_rows * group_rows * width,
        moved=6 * group_rows * width,
        name="returned",
        prefetch=1,
    )
    shares = lax.all_to_all(total.reshape(peers, group_rows // peers, width), "event", 0, 0, tiled=True)
    return jnp.sum(shares.astype(F32), axis=0)


def solution(mesh):
    in_specs = (
        P("node", None),
        P(("node", "event"), None, None, None),
        P(("node", "event"), None, None),
        P(("node", "event"), None, None),
        P(("node", "event"), None, None),
        P(("node", "event"), None, None),
        P(("node", "event"), None),
        P(("node", "event"), None, None),
        P(),
        P(),
        P(),
        P(),
        P(),
    )
    out_specs = P(("node", "event"), None)
    return jax.shard_map(local, mesh=mesh, in_specs=in_specs, out_specs=out_specs, check_vma=False)
```

```python
import functools

import jax
import jax.numpy as jnp
from jax import lax
from jax.experimental import pallas as pl
from jax.experimental.pallas import tpu as pltpu
from jax.sharding import PartitionSpec as P

F32 = jnp.float32
BF16 = jnp.bfloat16


def dot(a, b):
    return jnp.dot(a, b, preferred_element_type=F32)


def dot_nt(a, b):
    return lax.dot_general(a, b, (((1,), (1,)), ((), ())), preferred_element_type=F32)


def iota(shape, dim):
    return lax.broadcasted_iota(jnp.int32, shape, dim)


def split(x):
    high = x.astype(BF16)
    low = (x - high.astype(F32)).astype(BF16)
    return high, low


def call(kernel, outs, args, grid=None, in_specs=None, out_specs=None, scratch=(), flops=0, moved=0, trans=0, name=None, prefetch=0, vmem=64):
    spec = pltpu.PrefetchScalarGridSpec(
        num_scalar_prefetch=prefetch,
        grid=grid or (1,),
        in_specs=in_specs,
        out_specs=out_specs,
        scratch_shapes=list(scratch),
    )
    return pl.pallas_call(
        kernel,
        out_shape=outs,
        grid_spec=spec,
        name=name,
        compiler_params=pltpu.CompilerParams(vmem_limit_bytes=min(vmem << 20, 67043328)),
        cost_estimate=pl.CostEstimate(flops=int(flops), bytes_accessed=int(moved), transcendentals=int(trans)),
    )(*args)


def whole(shape):
    return pl.BlockSpec(shape, lambda *_: (0,) * len(shape))


def pack_kernel(group_rows, table_rows, feat, source, partner, negative, time, count, wanted, out):
    shards, slots, width = feat.shape
    groups = wanted.shape[0]
    live = iota((slots, shards), 0) < count[...]
    fields = (
        jnp.where(live, source[...], group_rows),
        jnp.where(live, partner[...], table_rows),
        jnp.where(live, negative[...], table_rows),
        time[...],
    )
    parts = []
    for field in fields:
        parts += [(field >> 8).astype(F32), (field & 255).astype(F32)]
    ids = jnp.concatenate(parts, axis=0).T
    rows = (shards, 8, width)

    def spread(x):
        return jnp.broadcast_to(x[:, None, :], rows)

    def by_group(x):
        return jnp.broadcast_to(x[:, None, :], (groups, shards // groups, width)).reshape(shards, width)

    place = iota(rows, 1)
    high = by_group((wanted[...] >> 8).astype(F32))
    low = by_group((wanted[...] & 255).astype(F32))
    tail = jnp.where(place == 0, spread(ids), jnp.where(place == 1, spread(high), spread(low)))
    out[:, 0:slots, :] = feat[...]
    out[:, slots : slots + 8, :] = tail.astype(BF16)


def field_columns(tail, field):
    blocks = tail.shape[0]
    row = tail[...].astype(F32)[:, 0:1, :]
    spread = jnp.broadcast_to(row, (blocks, 16, 128)).reshape(blocks * 16, 128)
    shape = (blocks * 16, 128)
    masked = jnp.where((iota(shape, 1) & 15) == (iota(shape, 0) & 15), spread, 0.0).astype(BF16)
    lane = iota((128, 128), 0) >> 4
    weight = jnp.where(lane == 2 * field, 256.0, jnp.where(lane == 2 * field + 1, 1.0, 0.0)).astype(BF16)
    return masked, weight


def columns_of(masked, weight):
    return dot(masked, weight)


def rows_of(masked, weight):
    return dot_nt(weight.T[0:8, :], masked)


def one_hot_columns(values, count):
    rows = values.shape[0]
    ids = values.astype(jnp.int32)
    pieces = [
        jnp.where(iota((rows, 128), 1) == ids - 128 * t, 1.0, 0.0).astype(BF16) for t in range(count // 128)
    ]
    return jnp.concatenate(pieces, axis=1)


def one_hot_rows(values, count, start=0):
    shape = (count, values.shape[1])
    ids = jnp.broadcast_to(values.astype(jnp.int32) - start, shape)
    return jnp.where(iota(shape, 0) == ids, 1.0, 0.0).astype(BF16)


def wanted_values(tail):
    rows = tail[...].astype(F32)[:, 0]
    return rows[:, 1], rows[:, 2]


def fetch_kernel(place, tail, memory, out):
    high, low = wanted_values(tail)
    groups = high.shape[0]
    shape = (groups * 128, 128)
    here = iota(shape, 1) == (iota(shape, 0) & 127)

    def spread(x):
        wide = jnp.broadcast_to(x[:, None, :], (groups, 128, 128)).reshape(shape)
        return jnp.where(here, wide, 0.0).astype(BF16)

    joined = jnp.concatenate([spread(high), spread(low)], axis=1)
    weight = jnp.where(iota((256, 128), 0) < 128, 256.0, 1.0).astype(BF16)
    values = dot(joined, weight)
    selector = one_hot_columns(values, memory.shape[0])
    out[...] = dot(selector, memory[...]).astype(BF16)


def source_kernel(tail, memory, freq, current, timing, rows):
    masked, weight = field_columns(tail, 0)
    values = columns_of(masked, weight)
    rows[...] = rows_of(masked, weight)
    selector = one_hot_columns(values, memory.shape[0])
    current[...] = dot(selector, memory[...]).astype(BF16)
    _, weight = field_columns(tail, 3)
    timing[...] = jnp.cos(columns_of(masked, weight) * freq[...]).astype(BF16)


def step_kernel(message, table, current_ref, timing, w_input, w_state, w_pair, bias, table_grad, grad_high, grad_low, acc, acc_neg):
    at = pl.program_id(0)
    table_rows, width = table.shape
    blocks = message.shape[0]
    events = blocks * 16
    feature = message[:, 0:16, :].reshape(events, 128)
    tail = message[:, 16:24, :]
    masked, weight_p = field_columns(tail, 1)
    _, weight_n = field_columns(tail, 2)
    partner = dot(one_hot_columns(columns_of(masked, weight_p), table_rows), table[...]).astype(BF16)
    negative = dot(one_hot_columns(columns_of(masked, weight_n), table_rows), table[...]).astype(BF16)
    current = current_ref[...]
    joined = jnp.concatenate([partner, feature, timing[...]], axis=1)
    w_in = w_input[...]
    from_input = dot(joined, w_in)
    from_state = dot(current, w_state[...])
    gate = bias[...]
    reset = jax.nn.sigmoid(from_input[:, :width] + from_state[:, :width] + gate[:, :width])
    update = jax.nn.sigmoid(
        from_input[:, width : 2 * width] + from_state[:, width : 2 * width] + gate[:, width : 2 * width]
    )
    recurrent = from_state[:, 2 * width :]
    candidate = jnp.tanh(from_input[:, 2 * width :] + gate[:, 2 * width :] + reset * recurrent)
    previous = current.astype(F32)
    renewed = (1.0 - update) * candidate + update * previous
    factor = 1.0 / width**0.5
    key_pos = dot(partner, w_pair[...])
    key_neg = dot(negative, w_pair[...])
    score_pos = jnp.sum(renewed * key_pos, axis=1, keepdims=True) * factor
    score_neg = jnp.sum(renewed * key_neg, axis=1, keepdims=True) * factor
    weight_pos = -jax.nn.sigmoid(-score_pos)
    weight_neg = jax.nn.sigmoid(score_neg)
    grad_renewed = (weight_pos * key_pos + weight_neg * key_neg) * factor
    grad_keypos = (weight_pos * renewed * factor).astype(BF16)
    grad_keyneg = (weight_neg * renewed * factor).astype(BF16)
    grad_cand = grad_renewed * (1.0 - update) * (1.0 - candidate * candidate)
    grad_reset = grad_cand * recurrent * reset * (1.0 - reset)
    grad_update = grad_renewed * (previous - candidate) * update * (1.0 - update)
    first = grad_reset.astype(BF16)
    second = grad_update.astype(BF16)
    input_back = jnp.concatenate([first, second, grad_cand.astype(BF16)], axis=1)
    state_back = jnp.concatenate([first, second, (grad_cand * reset).astype(BF16)], axis=1)
    grad_current = grad_renewed * update + dot_nt(state_back, w_state[...])
    high, low = split(grad_current)
    grad_high[...] = high
    grad_low[...] = low
    grad_partner = dot_nt(input_back, w_in[:width, :]) + dot_nt(grad_keypos, w_pair[...])
    high, low = split(grad_partner)
    to_partner = one_hot_rows(rows_of(masked, weight_p)[0:1, :], table_rows)
    to_negative = one_hot_rows(rows_of(masked, weight_n)[0:1, :], table_rows)
    added = dot(to_partner, high) + dot(to_partner, low)
    added_neg = dot(to_negative, grad_keyneg)

    @pl.when(at == 0)
    def _():
        acc[...] = added
        acc_neg[...] = added_neg

    @pl.when(at > 0)
    def _():
        acc[...] += added
        acc_neg[...] += added_neg

    @pl.when(at == pl.num_programs(0) - 1)
    def _():
        high, low = split(acc_neg[...])
        total = acc[...] + dot_nt(high, w_pair[...]) + dot_nt(low, w_pair[...])
        table_grad[...] = total.astype(BF16)


def source_scatter_kernel(rows, grad_high, grad_low, out):
    count = out.shape[0]
    selector = one_hot_rows(rows[0:1, :], count, pl.program_id(0) * count)
    out[...] = dot(selector, grad_high[...]) + dot(selector, grad_low[...])


def returned_kernel(place, tail, returned, state_grad, out):
    high, low = wanted_values(tail)
    values = high * 256.0 + low
    count = out.shape[0]
    start = pl.program_id(0) * count
    pieces = [one_hot_rows(values[g : g + 1, :], count, start) for g in range(values.shape[0])]
    selector = jnp.concatenate(pieces, axis=1)
    out[...] = (state_grad[...] + dot(selector, returned[...])).astype(BF16)


def local(
    memory,
    event_feat,
    event_source,
    event_partner,
    event_negative,
    event_time,
    event_count,
    requests,
    w_input,
    w_state,
    w_pair,
    gate_bias,
    time_freq,
):
    nodes = lax.axis_size("node")
    peers = lax.axis_size("event")
    shards = nodes * peers
    group_rows, width = memory.shape
    _, groups, per_group = requests.shape
    table_rows = groups * per_group
    slots, feat_width = event_feat.shape[2:]
    events = shards * slots

    flat = [x[0].T for x in (event_source, event_partner, event_negative, event_time)]
    args = (event_feat[0], *flat, event_count, requests[0])
    message = call(
        functools.partial(pack_kernel, group_rows, table_rows),
        jax.ShapeDtypeStruct((shards, slots + 8, feat_width), BF16),
        args,
        in_specs=[whole(x.shape) for x in args],
        out_specs=whole((shards, slots + 8, feat_width)),
        moved=2 * events * feat_width * 2,
        name="pack",
    )
    message = lax.all_to_all(message, ("node", "event"), 0, 0, tiled=True)
    place = lax.axis_index("event").astype(jnp.int32).reshape(1)
    by_peer = message.reshape(nodes, peers, slots + 8, feat_width)
    tail_spec = pl.BlockSpec((nodes, 1, 8, feat_width), lambda i, at: (0, at[0], slots // 8, 0))
    fetched = call(
        fetch_kernel,
        jax.ShapeDtypeStruct((table_rows, width), BF16),
        (place, by_peer, memory),
        in_specs=[tail_spec, whole(memory.shape)],
        out_specs=whole((table_rows, width)),
        flops=2 * table_rows * group_rows * width,
        moved=group_rows * width * 2,
        name="fetch",
        prefetch=1,
    )
    table = lax.all_to_all(fetched.reshape(groups, per_group, width), "node", 0, 0, tiled=True).reshape(table_rows, width)

    block = 512
    turns = events // block
    rows_block = lambda i: (i, 0)
    current, timing, rows = call(
        source_kernel,
        (
            jax.ShapeDtypeStruct((events, width), BF16),
            jax.ShapeDtypeStruct((events, feat_width), BF16),
            jax.ShapeDtypeStruct((8, events), F32),
        ),
        (message, memory, time_freq.reshape(1, -1)),
        grid=(turns,),
        in_specs=[
            pl.BlockSpec((block // slots, 8, feat_width), lambda i: (i, slots // 8, 0)),
            whole(memory.shape),
            whole((1, feat_width)),
        ],
        out_specs=(
            pl.BlockSpec((block, width), rows_block),
            pl.BlockSpec((block, feat_width), rows_block),
            pl.BlockSpec((8, block), lambda i: (0, i)),
        ),
        flops=2 * events * group_rows * width,
        moved=4 * events * width,
        trans=events * feat_width,
        name="source",
    )
    table_grad, grad_high, grad_low = call(
        step_kernel,
        (
            jax.ShapeDtypeStruct((table_rows, width), BF16),
            jax.ShapeDtypeStruct((events, width), BF16),
            jax.ShapeDtypeStruct((events, width), BF16),
        ),
        (message, table, current, timing, w_input, w_state, w_pair, gate_bias.reshape(1, -1)),
        grid=(turns,),
        in_specs=[
            pl.BlockSpec((block // slots, slots + 8, feat_width), lambda i: (i, 0, 0)),
            whole(table.shape),
            pl.BlockSpec((block, width), rows_block),
            pl.BlockSpec((block, feat_width), rows_block),
            whole(w_input.shape),
            whole(w_state.shape),
            whole(w_pair.shape),
            whole((1, 3 * width)),
        ],
        out_specs=(
            whole((table_rows, width)),
            pl.BlockSpec((block, width), rows_block),
            pl.BlockSpec((block, width), rows_block),
        ),
        scratch=[pltpu.VMEM((table_rows, width), F32), pltpu.VMEM((table_rows, width), F32)],
        flops=2 * events * width * (5 * table_rows + 3 * 4 * width + 3 * 3 * width),
        moved=8 * events * width,
        trans=events * width * 3,
        name="step",
    )
    returned = lax.all_to_all(table_grad.reshape(groups, per_group, width), "node", 0, 0, tiled=True).reshape(table_rows, width)
    node_block = 512
    state_grad = call(
        source_scatter_kernel,
        jax.ShapeDtypeStruct((group_rows, width), F32),
        (rows, grad_high, grad_low),
        grid=(group_rows // node_block,),
        in_specs=[whole(rows.shape), whole(grad_high.shape), whole(grad_low.shape)],
        out_specs=pl.BlockSpec((node_block, width), rows_block),
        flops=4 * events * group_rows * width,
        moved=8 * events * width,
        name="scatter",
    )
    total = call(
        returned_kernel,
        jax.ShapeDtypeStruct((group_rows, width), BF16),
        (place, by_peer, returned, state_grad),
        grid=(group_rows // node_block,),
        in_specs=[
            tail_spec,
            pl.BlockSpec((table_rows, width), lambda i, at: (0, 0)),
            pl.BlockSpec((node_block, width), lambda i, at: (i, 0)),
        ],
        out_specs=pl.BlockSpec((node_block, width), lambda i, at: (i, 0)),
        flops=2 * table_rows * group_rows * width,
        moved=6 * group_rows * width,
        name="returned",
        prefetch=1,
    )
    shares = lax.all_to_all(total.reshape(peers, group_rows // peers, width), "event", 0, 0, tiled=True)
    return jnp.sum(shares.astype(F32), axis=0)


def solution(mesh):
    in_specs = (
        P("node", None),
        P(("node", "event"), None, None, None),
        P(("node", "event"), None, None),
        P(("node", "event"), None, None),
        P(("node", "event"), None, None),
        P(("node", "event"), None, None),
        P(("node", "event"), None),
        P(("node", "event"), None, None),
        P(),
        P(),
        P(),
        P(),
        P(),
    )
    out_specs = P(("node", "event"), None)
    return jax.shard_map(local, mesh=mesh, in_specs=in_specs, out_specs=out_specs, check_vma=False)
```

```python
import functools
import math

import jax
import jax.numpy as jnp
from jax import lax
from jax.experimental import pallas as pl
from jax.experimental.pallas import tpu as pltpu
from jax.sharding import PartitionSpec as P

F32 = jnp.float32
BF16 = jnp.bfloat16
STEP_BLOCK = 1024
STEP_PARTS = 2
PI_HIGH = 3.140625
PI_LOW = math.pi - PI_HIGH


def dot(a, b):
    return jnp.dot(a, b, preferred_element_type=F32)


def dot_nt(a, b):
    return lax.dot_general(a, b, (((1,), (1,)), ((), ())), preferred_element_type=F32)


def iota(shape, dim):
    return lax.broadcasted_iota(jnp.int32, shape, dim)


def split(x):
    high = x.astype(BF16)
    low = (x - high.astype(F32)).astype(BF16)
    return high, low


def call(kernel, outs, args, grid=None, in_specs=None, out_specs=None, scratch=(), flops=0, moved=0, trans=0, name=None, prefetch=0, vmem=64, flags=None):
    spec = pltpu.PrefetchScalarGridSpec(
        num_scalar_prefetch=prefetch,
        grid=grid or (1,),
        in_specs=in_specs,
        out_specs=out_specs,
        scratch_shapes=list(scratch),
    )
    return pl.pallas_call(
        kernel,
        out_shape=outs,
        grid_spec=spec,
        name=name,
        compiler_params=pltpu.CompilerParams(vmem_limit_bytes=min(vmem << 20, 67043328), flags=flags),
        cost_estimate=pl.CostEstimate(flops=int(flops), bytes_accessed=int(moved), transcendentals=int(trans)),
    )(*args)


def whole(shape):
    return pl.BlockSpec(shape, lambda *_: (0,) * len(shape))


def pack_kernel(group_rows, table_rows, feat, source, partner, negative, time, count, wanted, out):
    shards, slots, width = feat.shape
    groups = wanted.shape[0]
    live = iota((slots, shards), 0) < count[...]
    fields = (
        jnp.where(live, source[...], group_rows),
        jnp.where(live, partner[...], table_rows),
        jnp.where(live, negative[...], table_rows),
        time[...],
    )
    parts = []
    for field in fields:
        parts += [(field >> 8).astype(F32), (field & 255).astype(F32)]
    ids = jnp.concatenate(parts, axis=0).T
    rows = (shards, 8, width)

    def spread(x):
        return jnp.broadcast_to(x[:, None, :], rows)

    def by_group(x):
        return jnp.broadcast_to(x[:, None, :], (groups, shards // groups, width)).reshape(shards, width)

    place = iota(rows, 1)
    high = by_group((wanted[...] >> 8).astype(F32))
    low = by_group((wanted[...] & 255).astype(F32))
    tail = jnp.where(place == 0, spread(ids), jnp.where(place == 1, spread(high), spread(low)))
    out[:, 0:slots, :] = feat[...]
    out[:, slots : slots + 8, :] = tail.astype(BF16)


def field_events(tail):
    blocks = tail.shape[0]
    row = tail[...].astype(F32)[:, 0:1, :]
    shape = (blocks * 16, 128)
    spread = jnp.broadcast_to(row, (blocks, 16, 128)).reshape(shape)
    return jnp.where((iota(shape, 1) & 15) == (iota(shape, 0) & 15), spread, 0.0).astype(BF16)


def columns_of(masked, field):
    lane = iota((128, 256), 0) >> 4
    part = iota((128, 256), 1) >> 7
    weight = jnp.where(lane == 2 * field + part, 1.0, 0.0).astype(BF16)
    both = dot(masked, weight).astype(BF16)
    return both[:, :128], both[:, 128:]


def rows_of(masked, fields):
    shape = (16 * fields, 128)
    weight = jnp.where(iota(shape, 1) >> 4 == iota(shape, 0) >> 3, 1.0, 0.0).astype(BF16)
    return dot_nt(weight, masked).astype(BF16)


def one_hot_columns(high, low, count):
    rows = low.shape[0]
    one, zero, none = (jnp.full((rows, 128), x, BF16) for x in (1.0, 0.0, -1.0))
    lanes = [(iota((rows, 128), 1) + 128 * t).astype(F32).astype(BF16) for t in range(2)]
    pieces = []
    for block in range(count // 256):
        key = jnp.where(high == jnp.full((rows, 128), block, BF16), low, none)
        pieces += [jnp.where(lane == key, one, zero) for lane in lanes]
    return jnp.concatenate(pieces, axis=1)


def one_hot_rows(high, low, count, start=0):
    events = low.shape[1]
    shape = (256, events)
    one, zero = jnp.full(shape, 1.0, BF16), jnp.full(shape, 0.0, BF16)
    place = iota(shape, 0).astype(F32).astype(BF16)
    pieces = []
    for block in range(count // 256):
        number = jnp.asarray(start + block, jnp.int32).astype(F32).astype(BF16)
        key = jnp.where(high == jnp.full((1, events), number, BF16), low, jnp.full((1, events), -1.0, BF16))
        pieces.append(jnp.where(place == jnp.broadcast_to(key, shape), one, zero))
    return jnp.concatenate(pieces, axis=0)


def wanted_values(tail):
    rows = tail[...].astype(F32)[:, 0]
    return rows[:, 1], rows[:, 2]


def fetch_kernel(place, tail, memory, out):
    high, low = wanted_values(tail)
    groups = high.shape[0]
    shape = (groups * 128, 128)
    here = iota(shape, 1) == (iota(shape, 0) & 127)

    def spread(x):
        wide = jnp.broadcast_to(x[:, None, :], (groups, 128, 128)).reshape(shape)
        return jnp.where(here, wide, 0.0).astype(BF16)

    ones = jnp.full((128, 128), 1.0, BF16)
    high, low = (dot(spread(x), ones).astype(BF16) for x in (high, low))
    selector = one_hot_columns(high, low, memory.shape[0])
    out[...] = dot(selector, memory[...]).astype(BF16)


def cosine(x):
    turns = jnp.floor(x * (0.5 / math.pi) + 0.5)
    rest = x * 0.5 - turns * PI_HIGH
    rest = rest - turns * PI_LOW
    square = rest * rest
    series = jnp.full_like(x, 1.0 / math.factorial(13))
    for power in (11, 9, 7, 5, 3, 1):
        series = series * square + (-1.0) ** (power // 2) / math.factorial(power)
    sine = series * rest
    return 1.0 - 2.0 * (sine * sine)


def source_kernel(tail, memory, freq, current, timing, rows):
    masked = field_events(tail)
    rows[...] = rows_of(masked, rows.shape[0] // 16)
    selector = one_hot_columns(*columns_of(masked, 0), memory.shape[0])
    current[...] = dot(selector, memory[...]).astype(BF16)
    high, low = columns_of(masked, 3)
    timing[...] = cosine((high.astype(F32) * 256.0 + low.astype(F32)) * freq[...]).astype(BF16)


def step_kernel(parts, message, table, current_ref, timing, rows, w_input, w_state, w_pair, bias, table_grad, grad_high, grad_low, acc, acc_neg):
    at = pl.program_id(0)
    table_rows, width = table.shape
    blocks = message.shape[0] // parts
    events = blocks * 16
    factor = 1.0 / width**0.5
    w_in, w_rec, pair = w_input[...], w_state[...], w_pair[...]
    w_gates = jnp.concatenate([w_in[:, : 2 * width], w_rec[:, : 2 * width]], axis=0)
    w_back = jnp.concatenate([w_in[:width, :], pair], axis=1)
    gate = bias[...].reshape(1, -1)

    def one_part(part):
        span = pl.ds(part * events, events)
        mine = message[part * blocks : (part + 1) * blocks]
        feature = mine[:, 0:16, :].reshape(events, 128)
        masked = field_events(mine[:, 16:24, :])
        partner = dot(one_hot_columns(*columns_of(masked, 1), table_rows), table[...]).astype(BF16)
        negative = dot(one_hot_columns(*columns_of(masked, 2), table_rows), table[...]).astype(BF16)
        current = current_ref[span, :]
        joined = jnp.concatenate([partner, feature, timing[span, :]], axis=1)
        gates = dot(jnp.concatenate([joined, current], axis=1), w_gates) + gate[:, : 2 * width]
        reset = jax.nn.sigmoid(gates[:, :width])
        update = jax.nn.sigmoid(gates[:, width:])
        recurrent = dot(current, w_rec[:, 2 * width :])
        candidate = jnp.tanh(dot(joined, w_in[:, 2 * width :]) + gate[:, 2 * width :] + reset * recurrent)
        previous = current.astype(F32)
        change = previous - candidate
        renewed = candidate + update * change
        key_pos = dot(partner, pair)
        key_neg = dot(negative, pair)
        score_pos = jnp.sum(renewed * key_pos, axis=1, keepdims=True) * factor
        score_neg = jnp.sum(renewed * key_neg, axis=1, keepdims=True) * factor
        weight_pos = jax.nn.sigmoid(-score_pos) * -factor
        weight_neg = jax.nn.sigmoid(score_neg) * factor
        grad_renewed = weight_pos * key_pos + weight_neg * key_neg
        grad_keypos = (weight_pos * renewed).astype(BF16)
        grad_keyneg = (weight_neg * renewed).astype(BF16)
        through = grad_renewed * update
        grad_cand = (grad_renewed - through) * (1.0 - candidate * candidate)
        gated = grad_cand * reset
        grad_reset = (gated * recurrent * (1.0 - reset)).astype(BF16)
        grad_update = (through * change * (1.0 - update)).astype(BF16)
        input_back = jnp.concatenate([grad_reset, grad_update, grad_cand.astype(BF16), grad_keypos], axis=1)
        state_back = jnp.concatenate([grad_reset, grad_update, gated.astype(BF16)], axis=1)
        grad_current = through + dot_nt(state_back, w_rec)
        high, low = split(grad_current)
        grad_high[span, :] = high
        grad_low[span, :] = low
        high, low = split(dot_nt(input_back, w_back))
        to_partner = one_hot_rows(rows[16:17, span], rows[24:25, span], table_rows)
        to_negative = one_hot_rows(rows[32:33, span], rows[40:41, span], table_rows)
        return to_partner, high, low, to_negative, grad_keyneg

    done = [one_part(part) for part in range(parts)]
    left = [x[0] for x in done]
    added = dot(
        jnp.concatenate(left + left, axis=1), jnp.concatenate([x[1] for x in done] + [x[2] for x in done], axis=0)
    )
    added_neg = dot(jnp.concatenate([x[3] for x in done], axis=1), jnp.concatenate([x[4] for x in done], axis=0))

    @pl.when(at == 0)
    def _():
        acc[...] = added
        acc_neg[...] = added_neg

    @pl.when(at > 0)
    def _():
        acc[...] += added
        acc_neg[...] += added_neg

    @pl.when(at == pl.num_programs(0) - 1)
    def _():
        high, low = split(acc_neg[...])
        both = jnp.concatenate([high, low], axis=1)
        total = acc[...] + dot_nt(both, jnp.concatenate([pair, pair], axis=1))
        table_grad[...] = total.astype(BF16)


def source_scatter_kernel(rows, grad_high, grad_low, out):
    count = out.shape[0]
    selector = one_hot_rows(rows[0:1, :], rows[8:9, :], count, pl.program_id(0) * (count // 256))
    out[...] = dot(jnp.concatenate([selector] * 2, axis=1), jnp.concatenate([grad_high[...], grad_low[...]], axis=0))


def returned_kernel(place, tail, returned, state_grad, out):
    high, low = wanted_values(tail)
    high, low = high.astype(BF16), low.astype(BF16)
    count = out.shape[0]
    start = pl.program_id(0) * (count // 256)
    pieces = [one_hot_rows(high[g : g + 1, :], low[g : g + 1, :], count, start) for g in range(high.shape[0])]
    selector = jnp.concatenate(pieces, axis=1)
    out[...] = (state_grad[...] + dot(selector, returned[...])).astype(BF16)


def local(
    memory,
    event_feat,
    event_source,
    event_partner,
    event_negative,
    event_time,
    event_count,
    requests,
    w_input,
    w_state,
    w_pair,
    gate_bias,
    time_freq,
):
    nodes = lax.axis_size("node")
    peers = lax.axis_size("event")
    shards = nodes * peers
    group_rows, width = memory.shape
    _, groups, per_group = requests.shape
    table_rows = groups * per_group
    slots, feat_width = event_feat.shape[2:]
    events = shards * slots

    flat = [x[0].T for x in (event_source, event_partner, event_negative, event_time)]
    args = (event_feat[0], *flat, event_count, requests[0])
    message = call(
        functools.partial(pack_kernel, group_rows, table_rows),
        jax.ShapeDtypeStruct((shards, slots + 8, feat_width), BF16),
        args,
        in_specs=[whole(x.shape) for x in args],
        out_specs=whole((shards, slots + 8, feat_width)),
        moved=2 * events * feat_width * 2,
        name="pack",
    )
    message = lax.all_to_all(message, ("node", "event"), 0, 0, tiled=True)
    place = lax.axis_index("event").astype(jnp.int32).reshape(1)
    by_peer = message.reshape(nodes, peers, slots + 8, feat_width)
    tail_spec = pl.BlockSpec((nodes, 1, 8, feat_width), lambda i, at: (0, at[0], slots // 8, 0))
    fetched = call(
        fetch_kernel,
        jax.ShapeDtypeStruct((table_rows, width), BF16),
        (place, by_peer, memory),
        in_specs=[tail_spec, whole(memory.shape)],
        out_specs=whole((table_rows, width)),
        flops=2 * table_rows * group_rows * width,
        moved=group_rows * width * 2,
        name="fetch",
        prefetch=1,
    )
    table = lax.all_to_all(fetched.reshape(groups, per_group, width), "node", 0, 0, tiled=True).reshape(table_rows, width)

    block = 1024
    turns = events // block
    rows_block = lambda i: (i, 0)
    current, timing, rows = call(
        source_kernel,
        (
            jax.ShapeDtypeStruct((events, width), BF16),
            jax.ShapeDtypeStruct((events, feat_width), BF16),
            jax.ShapeDtypeStruct((48, events), BF16),
        ),
        (message, memory, time_freq.reshape(1, -1)),
        grid=(turns,),
        in_specs=[
            pl.BlockSpec((block // slots, 8, feat_width), lambda i: (i, slots // 8, 0)),
            whole(memory.shape),
            whole((1, feat_width)),
        ],
        out_specs=(
            pl.BlockSpec((block, width), rows_block),
            pl.BlockSpec((block, feat_width), rows_block),
            pl.BlockSpec((48, block), lambda i: (0, i)),
        ),
        flops=2 * events * group_rows * width,
        moved=4 * events * width,
        trans=events * feat_width,
        name="source",
    )
    block = STEP_BLOCK
    turns = events // block
    table_grad, grad_high, grad_low = call(
        functools.partial(step_kernel, STEP_PARTS),
        (
            jax.ShapeDtypeStruct((table_rows, width), BF16),
            jax.ShapeDtypeStruct((events, width), BF16),
            jax.ShapeDtypeStruct((events, width), BF16),
        ),
        (message, table, current, timing, rows, w_input, w_state, w_pair, gate_bias),
        grid=(turns,),
        in_specs=[
            pl.BlockSpec((block // slots, slots + 8, feat_width), lambda i: (i, 0, 0)),
            whole(table.shape),
            pl.BlockSpec((block, width), rows_block),
            pl.BlockSpec((block, feat_width), rows_block),
            pl.BlockSpec((48, block), lambda i: (0, i)),
            whole(w_input.shape),
            whole(w_state.shape),
            whole(w_pair.shape),
            whole((3 * width,)),
        ],
        out_specs=(
            whole((table_rows, width)),
            pl.BlockSpec((block, width), rows_block),
            pl.BlockSpec((block, width), rows_block),
        ),
        scratch=[pltpu.VMEM((table_rows, width), F32), pltpu.VMEM((table_rows, width), F32)],
        flops=2 * events * width * (5 * table_rows + 3 * 4 * width + 3 * 3 * width),
        moved=8 * events * width,
        trans=events * width * 3,
        name="step",
    )
    returned = lax.all_to_all(table_grad.reshape(groups, per_group, width), "node", 0, 0, tiled=True).reshape(table_rows, width)
    node_block = 1024
    state_grad = call(
        source_scatter_kernel,
        jax.ShapeDtypeStruct((group_rows, width), F32),
        (rows, grad_high, grad_low),
        grid=(group_rows // node_block,),
        in_specs=[whole((16, events)), whole(grad_high.shape), whole(grad_low.shape)],
        out_specs=pl.BlockSpec((node_block, width), rows_block),
        flops=4 * events * group_rows * width,
        moved=8 * events * width,
        name="scatter",
    )
    node_block = 1024
    total = call(
        returned_kernel,
        jax.ShapeDtypeStruct((group_rows, width), BF16),
        (place, by_peer, returned, state_grad),
        grid=(group_rows // node_block,),
        in_specs=[
            tail_spec,
            pl.BlockSpec((table_rows, width), lambda i, at: (0, 0)),
            pl.BlockSpec((node_block, width), lambda i, at: (i, 0)),
        ],
        out_specs=pl.BlockSpec((node_block, width), lambda i, at: (i, 0)),
        flops=2 * table_rows * group_rows * width,
        moved=6 * group_rows * width,
        name="returned",
        prefetch=1,
    )
    shares = lax.all_to_all(total.reshape(peers, group_rows // peers, width), "event", 0, 0, tiled=True)
    return jnp.sum(shares.astype(F32), axis=0)


def solution(mesh):
    in_specs = (
        P("node", None),
        P(("node", "event"), None, None, None),
        P(("node", "event"), None, None),
        P(("node", "event"), None, None),
        P(("node", "event"), None, None),
        P(("node", "event"), None, None),
        P(("node", "event"), None),
        P(("node", "event"), None, None),
        P(),
        P(),
        P(),
        P(),
        P(),
    )
    out_specs = P(("node", "event"), None)
    return jax.shard_map(local, mesh=mesh, in_specs=in_specs, out_specs=out_specs, check_vma=False)
```

```python
import functools
import math

import jax
import jax.numpy as jnp
from jax import lax
from jax.experimental import pallas as pl
from jax.experimental.pallas import tpu as pltpu
from jax.sharding import PartitionSpec as P

F32 = jnp.float32
BF16 = jnp.bfloat16
STEP_BLOCK = 1024
STEP_PARTS = 2
PI_HIGH = 3.140625
PI_LOW = math.pi - PI_HIGH


def dot(a, b):
    return jnp.dot(a, b, preferred_element_type=F32)


def dot_nt(a, b):
    return lax.dot_general(a, b, (((1,), (1,)), ((), ())), preferred_element_type=F32)


def iota(shape, dim):
    return lax.broadcasted_iota(jnp.int32, shape, dim)


def split(x):
    high = x.astype(BF16)
    low = (x - high.astype(F32)).astype(BF16)
    return high, low


def call(kernel, outs, args, grid=None, in_specs=None, out_specs=None, scratch=(), flops=0, moved=0, trans=0, name=None, prefetch=0, vmem=48, flags=None):
    spec = pltpu.PrefetchScalarGridSpec(
        num_scalar_prefetch=prefetch,
        grid=grid or (1,),
        in_specs=in_specs,
        out_specs=out_specs,
        scratch_shapes=list(scratch),
    )
    return pl.pallas_call(
        kernel,
        out_shape=outs,
        grid_spec=spec,
        name=name,
        compiler_params=pltpu.CompilerParams(vmem_limit_bytes=min(vmem << 20, 67043328), flags=flags),
        cost_estimate=pl.CostEstimate(flops=int(flops), bytes_accessed=int(moved), transcendentals=int(trans)),
    )(*args)


def in_hbm(x):
    return pltpu.with_memory_space_constraint(x, pltpu.HBM)


def whole(shape):
    return pl.BlockSpec(shape, lambda *_: (0,) * len(shape))


def pack_kernel(group_rows, table_rows, feat, source, partner, negative, time, count, wanted, out):
    shards, slots, width = feat.shape
    groups = wanted.shape[0]
    live = iota((slots, shards), 0) < count[...]
    fields = (
        jnp.where(live, source[...], group_rows),
        jnp.where(live, partner[...], table_rows),
        jnp.where(live, negative[...], table_rows),
        time[...],
    )
    parts = []
    for field in fields:
        parts += [(field >> 8).astype(F32), (field & 255).astype(F32)]
    ids = jnp.concatenate(parts, axis=0).T
    rows = (shards, 8, width)

    def spread(x):
        return jnp.broadcast_to(x[:, None, :], rows)

    def by_group(x):
        return jnp.broadcast_to(x[:, None, :], (groups, shards // groups, width)).reshape(shards, width)

    place = iota(rows, 1)
    high = by_group((wanted[...] >> 8).astype(F32))
    low = by_group((wanted[...] & 255).astype(F32))
    tail = jnp.where(place == 0, spread(ids), jnp.where(place == 1, spread(high), spread(low)))
    out[:, 0:slots, :] = feat[...]
    out[:, slots : slots + 8, :] = tail.astype(BF16)


def field_events(tail):
    blocks = tail.shape[0]
    row = tail[...].astype(F32)[:, 0:1, :]
    shape = (blocks * 16, 128)
    spread = jnp.broadcast_to(row, (blocks, 16, 128)).reshape(shape)
    return jnp.where((iota(shape, 1) & 15) == (iota(shape, 0) & 15), spread, 0.0).astype(BF16)


def columns_of(masked, field):
    lane = iota((128, 256), 0) >> 4
    part = iota((128, 256), 1) >> 7
    weight = jnp.where(lane == 2 * field + part, 1.0, 0.0).astype(BF16)
    both = dot(masked, weight).astype(BF16)
    return both[:, :128], both[:, 128:]


def rows_of(masked, fields):
    shape = (16 * fields, 128)
    weight = jnp.where(iota(shape, 1) >> 4 == iota(shape, 0) >> 3, 1.0, 0.0).astype(BF16)
    return dot_nt(weight, masked).astype(BF16)


def one_hot_columns(high, low, count):
    rows = low.shape[0]
    one, zero, none = (jnp.full((rows, 128), x, BF16) for x in (1.0, 0.0, -1.0))
    lanes = [(iota((rows, 128), 1) + 128 * t).astype(F32).astype(BF16) for t in range(2)]
    pieces = []
    for block in range(count // 256):
        key = jnp.where(high == jnp.full((rows, 128), block, BF16), low, none)
        pieces += [jnp.where(lane == key, one, zero) for lane in lanes]
    return jnp.concatenate(pieces, axis=1)


def one_hot_rows(high, low, count, start=0):
    events = low.shape[1]
    shape = (256, events)
    one, zero = jnp.full(shape, 1.0, BF16), jnp.full(shape, 0.0, BF16)
    place = iota(shape, 0).astype(F32).astype(BF16)
    pieces = []
    for block in range(count // 256):
        number = jnp.asarray(start + block, jnp.int32).astype(F32).astype(BF16)
        key = jnp.where(high == jnp.full((1, events), number, BF16), low, jnp.full((1, events), -1.0, BF16))
        pieces.append(jnp.where(place == jnp.broadcast_to(key, shape), one, zero))
    return jnp.concatenate(pieces, axis=0)


def wanted_values(tail):
    rows = tail[...].astype(F32)[:, 0]
    return rows[:, 1], rows[:, 2]


def fetch_kernel(place, tail, memory, out, wanted):
    high, low = wanted_values(tail)
    wanted[...] = jnp.concatenate([high, low], axis=0).astype(BF16)
    groups = high.shape[0]
    shape = (groups * 128, 128)
    here = iota(shape, 1) == (iota(shape, 0) & 127)

    def spread(x):
        wide = jnp.broadcast_to(x[:, None, :], (groups, 128, 128)).reshape(shape)
        return jnp.where(here, wide, 0.0).astype(BF16)

    ones = jnp.full((128, 128), 1.0, BF16)
    high, low = (dot(spread(x), ones).astype(BF16) for x in (high, low))
    selector = one_hot_columns(high, low, memory.shape[0])
    out[...] = dot(selector, memory[...]).astype(BF16)


def cosine(x):
    turns = jnp.floor(x * (0.5 / math.pi) + 0.5)
    rest = x * 0.5 - turns * PI_HIGH
    rest = rest - turns * PI_LOW
    square = rest * rest
    series = jnp.full_like(x, 1.0 / math.factorial(13))
    for power in (11, 9, 7, 5, 3, 1):
        series = series * square + (-1.0) ** (power // 2) / math.factorial(power)
    sine = series * rest
    return 1.0 - 2.0 * (sine * sine)


def source_kernel(tail, memory, freq, current, timing, rows):
    masked = field_events(tail)
    rows[...] = rows_of(masked, rows.shape[0] // 16)
    selector = one_hot_columns(*columns_of(masked, 0), memory.shape[0])
    current[...] = dot(selector, memory[...]).astype(BF16)
    high, low = columns_of(masked, 3)
    timing[...] = cosine((high.astype(F32) * 256.0 + low.astype(F32)) * freq[...]).astype(BF16)


def step_kernel(parts, message, table, current_ref, timing, rows, w_input, w_state, w_pair, bias, table_grad, grad_high, grad_low, acc, acc_neg):
    at = pl.program_id(0)
    table_rows, width = table.shape
    blocks = message.shape[0] // parts
    events = blocks * 16
    factor = 1.0 / width**0.5
    w_in, w_rec, pair = w_input[...], w_state[...], w_pair[...]
    w_gates = jnp.concatenate([w_in[:, : 2 * width], w_rec[:, : 2 * width]], axis=0)
    w_back = jnp.concatenate([w_in[:width, :], pair], axis=1)
    gate = bias[...].reshape(1, -1)

    def one_part(part):
        span = pl.ds(part * events, events)
        mine = message[part * blocks : (part + 1) * blocks]
        feature = mine[:, 0:16, :].reshape(events, 128)
        masked = field_events(mine[:, 16:24, :])
        partner = dot(one_hot_columns(*columns_of(masked, 1), table_rows), table[...]).astype(BF16)
        negative = dot(one_hot_columns(*columns_of(masked, 2), table_rows), table[...]).astype(BF16)
        current = current_ref[span, :]
        joined = jnp.concatenate([partner, feature, timing[span, :]], axis=1)
        gates = dot(jnp.concatenate([joined, current], axis=1), w_gates) + gate[:, : 2 * width]
        reset = jax.nn.sigmoid(gates[:, :width])
        update = jax.nn.sigmoid(gates[:, width:])
        recurrent = dot(current, w_rec[:, 2 * width :])
        candidate = jnp.tanh(dot(joined, w_in[:, 2 * width :]) + gate[:, 2 * width :] + reset * recurrent)
        previous = current.astype(F32)
        change = previous - candidate
        renewed = candidate + update * change
        key_pos = dot(partner, pair)
        key_neg = dot(negative, pair)
        score_pos = jnp.sum(renewed * key_pos, axis=1, keepdims=True) * factor
        score_neg = jnp.sum(renewed * key_neg, axis=1, keepdims=True) * factor
        weight_pos = jax.nn.sigmoid(-score_pos) * -factor
        weight_neg = jax.nn.sigmoid(score_neg) * factor
        grad_renewed = weight_pos * key_pos + weight_neg * key_neg
        grad_keypos = (weight_pos * renewed).astype(BF16)
        grad_keyneg = (weight_neg * renewed).astype(BF16)
        through = grad_renewed * update
        grad_cand = (grad_renewed - through) * (1.0 - candidate * candidate)
        gated = grad_cand * reset
        grad_reset = (gated * recurrent * (1.0 - reset)).astype(BF16)
        grad_update = (through * change * (1.0 - update)).astype(BF16)
        input_back = jnp.concatenate([grad_reset, grad_update, grad_cand.astype(BF16), grad_keypos], axis=1)
        state_back = jnp.concatenate([grad_reset, grad_update, gated.astype(BF16)], axis=1)
        grad_current = through + dot_nt(state_back, w_rec)
        high, low = split(grad_current)
        grad_high[span, :] = high
        grad_low[span, :] = low
        high, low = split(dot_nt(input_back, w_back))
        to_partner = one_hot_rows(rows[16:17, span], rows[24:25, span], table_rows)
        to_negative = one_hot_rows(rows[32:33, span], rows[40:41, span], table_rows)
        return to_partner, high, low, to_negative, grad_keyneg

    done = [one_part(part) for part in range(parts)]
    left = [x[0] for x in done]
    added = dot(
        jnp.concatenate(left + left, axis=1), jnp.concatenate([x[1] for x in done] + [x[2] for x in done], axis=0)
    )
    added_neg = dot(jnp.concatenate([x[3] for x in done], axis=1), jnp.concatenate([x[4] for x in done], axis=0))

    @pl.when(at == 0)
    def _():
        acc[...] = added
        acc_neg[...] = added_neg

    @pl.when(at > 0)
    def _():
        acc[...] += added
        acc_neg[...] += added_neg

    @pl.when(at == pl.num_programs(0) - 1)
    def _():
        high, low = split(acc_neg[...])
        both = jnp.concatenate([high, low], axis=1)
        total = acc[...] + dot_nt(both, jnp.concatenate([pair, pair], axis=1))
        table_grad[...] = total.astype(BF16)


def source_scatter_kernel(rows, grad_high, grad_low, out):
    count = out.shape[0]
    selector = one_hot_rows(rows[0:1, :], rows[8:9, :], count, pl.program_id(0) * (count // 256))
    out[...] = dot(jnp.concatenate([selector] * 2, axis=1), jnp.concatenate([grad_high[...], grad_low[...]], axis=0))


def returned_kernel(wanted, returned, state_grad, out):
    groups = wanted.shape[0] // 2
    high, low = wanted[0:groups, :], wanted[groups:, :]
    count = out.shape[0]
    start = pl.program_id(0) * (count // 256)
    pieces = [one_hot_rows(high[g : g + 1, :], low[g : g + 1, :], count, start) for g in range(high.shape[0])]
    selector = jnp.concatenate(pieces, axis=1)
    out[...] = (state_grad[...] + dot(selector, returned[...])).astype(BF16)


def local(
    memory,
    event_feat,
    event_source,
    event_partner,
    event_negative,
    event_time,
    event_count,
    requests,
    w_input,
    w_state,
    w_pair,
    gate_bias,
    time_freq,
):
    nodes = lax.axis_size("node")
    peers = lax.axis_size("event")
    shards = nodes * peers
    group_rows, width = memory.shape
    _, groups, per_group = requests.shape
    table_rows = groups * per_group
    slots, feat_width = event_feat.shape[2:]
    events = shards * slots

    w_input, w_state, w_pair, gate_bias, time_freq, memory = map(in_hbm, (w_input, w_state, w_pair, gate_bias, time_freq.reshape(1, -1), memory))
    flat = [x[0].T for x in (event_source, event_partner, event_negative, event_time)]
    args = (event_feat[0], *flat, event_count, requests[0])
    message = call(
        functools.partial(pack_kernel, group_rows, table_rows),
        jax.ShapeDtypeStruct((shards, slots + 8, feat_width), BF16),
        args,
        in_specs=[whole(x.shape) for x in args],
        out_specs=whole((shards, slots + 8, feat_width)),
        moved=2 * events * feat_width * 2,
        name="pack",
        vmem=64,
    )
    message = lax.all_to_all(message, ("node", "event"), 0, 0, tiled=True)
    place = lax.axis_index("event").astype(jnp.int32).reshape(1)
    by_peer = message.reshape(nodes, peers, slots + 8, feat_width)
    tail_spec = pl.BlockSpec((nodes, 1, 8, feat_width), lambda i, at: (0, at[0], slots // 8, 0))
    fetched, wanted = call(
        fetch_kernel,
        (jax.ShapeDtypeStruct((table_rows, width), BF16), jax.ShapeDtypeStruct((2 * groups, per_group), BF16)),
        (place, by_peer, memory),
        in_specs=[tail_spec, whole(memory.shape)],
        out_specs=(whole((table_rows, width)), whole((2 * groups, per_group))),
        flops=2 * table_rows * group_rows * width,
        moved=group_rows * width * 2,
        name="fetch",
        prefetch=1,
    )
    table = lax.all_to_all(fetched.reshape(groups, per_group, width), "node", 0, 0, tiled=True).reshape(table_rows, width)

    block = 1024
    turns = events // block
    rows_block = lambda i: (i, 0)
    current, timing, rows = call(
        source_kernel,
        (
            pltpu.HBM((events, width), BF16),
            jax.ShapeDtypeStruct((events, feat_width), BF16),
            jax.ShapeDtypeStruct((48, events), BF16),
        ),
        (message, memory, time_freq),
        grid=(turns,),
        in_specs=[
            pl.BlockSpec((block // slots, 8, feat_width), lambda i: (i, slots // 8, 0)),
            whole(memory.shape),
            whole((1, feat_width)),
        ],
        out_specs=(
            pl.BlockSpec((block, width), rows_block),
            pl.BlockSpec((block, feat_width), rows_block),
            pl.BlockSpec((48, block), lambda i: (0, i)),
        ),
        flops=2 * events * group_rows * width,
        moved=4 * events * width,
        trans=events * feat_width,
        name="source",
    )
    block = STEP_BLOCK
    turns = events // block
    table_grad, grad_high, grad_low = call(
        functools.partial(step_kernel, STEP_PARTS),
        (
            jax.ShapeDtypeStruct((table_rows, width), BF16),
            pltpu.HBM((events, width), BF16),
            pltpu.HBM((events, width), BF16),
        ),
        (message, table, in_hbm(current), timing, rows, w_input, w_state, w_pair, gate_bias),
        grid=(turns,),
        in_specs=[
            pl.BlockSpec((block // slots, slots + 8, feat_width), lambda i: (i, 0, 0)),
            whole(table.shape),
            pl.BlockSpec((block, width), rows_block),
            pl.BlockSpec((block, feat_width), rows_block),
            pl.BlockSpec((48, block), lambda i: (0, i)),
            whole(w_input.shape),
            whole(w_state.shape),
            whole(w_pair.shape),
            whole((3 * width,)),
        ],
        out_specs=(
            whole((table_rows, width)),
            pl.BlockSpec((block, width), rows_block),
            pl.BlockSpec((block, width), rows_block),
        ),
        scratch=[pltpu.VMEM((table_rows, width), F32), pltpu.VMEM((table_rows, width), F32)],
        flops=2 * events * width * (5 * table_rows + 3 * 4 * width + 3 * 3 * width),
        moved=8 * events * width,
        trans=events * width * 3,
        name="step",
    )
    returned = lax.all_to_all(table_grad.reshape(groups, per_group, width), "node", 0, 0, tiled=True).reshape(table_rows, width)
    node_block = 1024
    state_grad = call(
        source_scatter_kernel,
        jax.ShapeDtypeStruct((group_rows, width), F32),
        (rows, in_hbm(grad_high), in_hbm(grad_low)),
        grid=(group_rows // node_block,),
        in_specs=[whole((16, events)), whole(grad_high.shape), whole(grad_low.shape)],
        out_specs=pl.BlockSpec((node_block, width), rows_block),
        flops=4 * events * group_rows * width,
        moved=8 * events * width,
        name="scatter",
    )
    node_block = 1024
    total = call(
        returned_kernel,
        jax.ShapeDtypeStruct((group_rows, width), BF16),
        (wanted, returned, state_grad),
        grid=(group_rows // node_block,),
        in_specs=[whole(wanted.shape), whole((table_rows, width)), pl.BlockSpec((node_block, width), rows_block)],
        out_specs=pl.BlockSpec((node_block, width), rows_block),
        flops=2 * table_rows * group_rows * width,
        moved=6 * group_rows * width,
        name="returned",
    )
    shares = lax.all_to_all(total.reshape(peers, group_rows // peers, width), "event", 0, 0, tiled=True)
    return jnp.sum(shares.astype(F32), axis=0)


def solution(mesh):
    in_specs = (
        P("node", None),
        P(("node", "event"), None, None, None),
        P(("node", "event"), None, None),
        P(("node", "event"), None, None),
        P(("node", "event"), None, None),
        P(("node", "event"), None, None),
        P(("node", "event"), None),
        P(("node", "event"), None, None),
        P(),
        P(),
        P(),
        P(),
        P(),
    )
    out_specs = P(("node", "event"), None)
    return jax.shard_map(local, mesh=mesh, in_specs=in_specs, out_specs=out_specs, check_vma=False)
```

```python
import functools
import math

import jax
import jax.numpy as jnp
from jax import lax
from jax.experimental import pallas as pl
from jax.experimental.pallas import tpu as pltpu
from jax.sharding import PartitionSpec as P

F32 = jnp.float32
BF16 = jnp.bfloat16
STEP_PARTS = 4
PI_HIGH = 3.140625
PI_LOW = math.pi - PI_HIGH


def dot(a, b):
    return jnp.dot(a, b, preferred_element_type=F32)


def dot_nt(a, b):
    return lax.dot_general(a, b, (((1,), (1,)), ((), ())), preferred_element_type=F32)


def iota(shape, dim):
    return lax.broadcasted_iota(jnp.int32, shape, dim)


def split(x):
    high = x.astype(BF16)
    low = (x - high.astype(F32)).astype(BF16)
    return high, low


def call(kernel, outs, args, grid=None, in_specs=None, out_specs=None, scratch=(), flops=0, moved=0, trans=0, name=None, prefetch=0, vmem=48, flags=None):
    spec = pltpu.PrefetchScalarGridSpec(
        num_scalar_prefetch=prefetch,
        grid=grid or (1,),
        in_specs=in_specs,
        out_specs=out_specs,
        scratch_shapes=list(scratch),
    )
    return pl.pallas_call(
        kernel,
        out_shape=outs,
        grid_spec=spec,
        name=name,
        compiler_params=pltpu.CompilerParams(vmem_limit_bytes=min(vmem << 20, 67043328), flags=flags),
        cost_estimate=pl.CostEstimate(flops=int(flops), bytes_accessed=int(moved), transcendentals=int(trans)),
    )(*args)


def in_hbm(x):
    return pltpu.with_memory_space_constraint(x, pltpu.HBM)


def whole(shape):
    return pl.BlockSpec(shape, lambda *_: (0,) * len(shape))


def pack_kernel(group_rows, table_rows, feat, source, partner, negative, time, count, wanted, out):
    shards, slots, width = feat.shape
    groups = wanted.shape[0]
    live = iota((slots, shards), 0) < count[...]
    fields = (
        jnp.where(live, source[...], group_rows),
        jnp.where(live, partner[...], table_rows),
        jnp.where(live, negative[...], table_rows),
        time[...],
    )
    parts = []
    for field in fields:
        parts += [(field >> 8).astype(F32), (field & 255).astype(F32)]
    ids = jnp.concatenate(parts, axis=0).T
    rows = (shards, 8, width)

    def spread(x):
        return jnp.broadcast_to(x[:, None, :], rows)

    def by_group(x):
        return jnp.broadcast_to(x[:, None, :], (groups, shards // groups, width)).reshape(shards, width)

    place = iota(rows, 1)
    high = by_group((wanted[...] >> 8).astype(F32))
    low = by_group((wanted[...] & 255).astype(F32))
    tail = jnp.where(place == 0, spread(ids), jnp.where(place == 1, spread(high), spread(low)))
    out[:, 0:slots, :] = feat[...]
    out[:, slots : slots + 8, :] = tail.astype(BF16)


def field_events(tail):
    blocks = tail.shape[0]
    row = tail[...].astype(F32)[:, 0:1, :]
    shape = (blocks * 16, 128)
    spread = jnp.broadcast_to(row, (blocks, 16, 128)).reshape(shape)
    return jnp.where((iota(shape, 1) & 15) == (iota(shape, 0) & 15), spread, 0.0).astype(BF16)


def columns_of(masked, field):
    lane = iota((128, 256), 0) >> 4
    part = iota((128, 256), 1) >> 7
    weight = jnp.where(lane == 2 * field + part, 1.0, 0.0).astype(BF16)
    both = dot(masked, weight).astype(BF16)
    return both[:, :128], both[:, 128:]


def rows_of(masked, fields):
    shape = (16 * fields, 128)
    weight = jnp.where(iota(shape, 1) >> 4 == iota(shape, 0) >> 3, 1.0, 0.0).astype(BF16)
    return dot_nt(weight, masked).astype(BF16)


def one_hot_columns(high, low, count):
    rows = low.shape[0]
    one, zero, none = (jnp.full((rows, 128), x, BF16) for x in (1.0, 0.0, -1.0))
    lanes = [(iota((rows, 128), 1) + 128 * t).astype(F32).astype(BF16) for t in range(2)]
    pieces = []
    for block in range(count // 256):
        key = jnp.where(high == jnp.full((rows, 128), block, BF16), low, none)
        pieces += [jnp.where(lane == key, one, zero) for lane in lanes]
    return jnp.concatenate(pieces, axis=1)


def one_hot_rows(high, low, count, start=0):
    events = low.shape[1]
    shape = (256, events)
    one, zero = jnp.full(shape, 1.0, BF16), jnp.full(shape, 0.0, BF16)
    place = iota(shape, 0).astype(F32).astype(BF16)
    pieces = []
    for block in range(count // 256):
        number = jnp.asarray(start + block, jnp.int32).astype(F32).astype(BF16)
        key = jnp.where(high == jnp.full((1, events), number, BF16), low, jnp.full((1, events), -1.0, BF16))
        pieces.append(jnp.where(place == jnp.broadcast_to(key, shape), one, zero))
    return jnp.concatenate(pieces, axis=0)


def wanted_values(tail):
    rows = tail[...].astype(F32)[:, 0]
    return rows[:, 1], rows[:, 2]


def fetch_kernel(place, tail, memory, out, wanted):
    high, low = wanted_values(tail)
    wanted[...] = jnp.concatenate([high, low], axis=0).astype(BF16)
    groups = high.shape[0]
    shape = (groups * 128, 128)
    here = iota(shape, 1) == (iota(shape, 0) & 127)

    def spread(x):
        wide = jnp.broadcast_to(x[:, None, :], (groups, 128, 128)).reshape(shape)
        return jnp.where(here, wide, 0.0).astype(BF16)

    ones = jnp.full((128, 128), 1.0, BF16)
    high, low = (dot(spread(x), ones).astype(BF16) for x in (high, low))
    selector = one_hot_columns(high, low, memory.shape[0])
    out[...] = dot(selector, memory[...]).astype(BF16)


def cosine(x):
    turns = jnp.floor(x * (0.5 / math.pi) + 0.5)
    rest = x * 0.5 - turns * PI_HIGH
    rest = rest - turns * PI_LOW
    square = rest * rest
    series = jnp.full_like(x, 1.0 / math.factorial(13))
    for power in (11, 9, 7, 5, 3, 1):
        series = series * square + (-1.0) ** (power // 2) / math.factorial(power)
    sine = series * rest
    return 1.0 - 2.0 * (sine * sine)


def source_kernel(tail, memory, freq, current, timing, rows):
    masked = field_events(tail)
    rows[...] = rows_of(masked, rows.shape[0] // 16)
    selector = one_hot_columns(*columns_of(masked, 0), memory.shape[0])
    current[...] = dot(selector, memory[...]).astype(BF16)
    high, low = columns_of(masked, 3)
    timing[...] = cosine((high.astype(F32) * 256.0 + low.astype(F32)) * freq[...]).astype(BF16)


def step_kernel(
    parts,
    message,
    table,
    timing,
    rows,
    bias,
    current_hbm,
    w_input_hbm,
    w_state_hbm,
    w_pair_hbm,
    table_grad,
    grad_high_hbm,
    grad_low_hbm,
    acc,
    acc_neg,
    current_ref,
    w_input,
    w_state,
    w_pair,
    grad_high,
    grad_low,
    sems,
):
    table_rows, width = table.shape
    blocks = message.shape[0] // parts
    events = blocks * 16
    factor = 1.0 / width**0.5
    reads = [
        pltpu.make_async_copy(a, b, sems.at[i])
        for i, (a, b) in enumerate(
            ((w_input_hbm, w_input), (w_state_hbm, w_state), (w_pair_hbm, w_pair), (current_hbm, current_ref))
        )
    ]
    writes = [
        pltpu.make_async_copy(a, b, sems.at[len(reads) + i])
        for i, (a, b) in enumerate(((grad_high, grad_high_hbm), (grad_low, grad_low_hbm)))
    ]
    for copy in reads:
        copy.start()

    def rows_for(part):
        mine = message[part * blocks : (part + 1) * blocks]
        masked = field_events(mine[:, 16:24, :])
        partner = dot(one_hot_columns(*columns_of(masked, 1), table_rows), table[...]).astype(BF16)
        negative = dot(one_hot_columns(*columns_of(masked, 2), table_rows), table[...]).astype(BF16)
        return mine[:, 0:16, :].reshape(events, 128), partner, negative

    first_rows = rows_for(0)
    for copy in reads:
        copy.wait()
    w_in, w_rec, pair = w_input[...], w_state[...], w_pair[...]
    w_gates = jnp.concatenate([w_in[:, : 2 * width], w_rec[:, : 2 * width]], axis=0)
    w_back = jnp.concatenate([w_in[:width, :], pair], axis=1)
    gate = bias[...].reshape(1, -1)

    def one_part(part):
        span = pl.ds(part * events, events)
        feature, partner, negative = rows_for(part) if part else first_rows
        current = current_ref[span, :]
        joined = jnp.concatenate([partner, feature, timing[span, :]], axis=1)
        gates = dot(jnp.concatenate([joined, current], axis=1), w_gates) + gate[:, : 2 * width]
        reset = jax.nn.sigmoid(gates[:, :width])
        update = jax.nn.sigmoid(gates[:, width:])
        recurrent = dot(current, w_rec[:, 2 * width :])
        candidate = jnp.tanh(dot(joined, w_in[:, 2 * width :]) + gate[:, 2 * width :] + reset * recurrent)
        change = current.astype(F32) - candidate
        renewed = candidate + update * change
        key_pos = dot(partner, pair)
        key_neg = dot(negative, pair)
        score_pos = jnp.sum(renewed * key_pos, axis=1, keepdims=True) * factor
        score_neg = jnp.sum(renewed * key_neg, axis=1, keepdims=True) * factor
        weight_pos = jax.nn.sigmoid(-score_pos) * -factor
        weight_neg = jax.nn.sigmoid(score_neg) * factor
        grad_renewed = weight_pos * key_pos + weight_neg * key_neg
        grad_keypos = (weight_pos * renewed).astype(BF16)
        grad_keyneg = (weight_neg * renewed).astype(BF16)
        through = grad_renewed * update
        grad_cand = (grad_renewed - through) * (1.0 - candidate * candidate)
        gated = grad_cand * reset
        grad_reset = (gated * recurrent * (1.0 - reset)).astype(BF16)
        grad_update = (through * change * (1.0 - update)).astype(BF16)
        input_back = jnp.concatenate([grad_reset, grad_update, grad_cand.astype(BF16), grad_keypos], axis=1)
        state_back = jnp.concatenate([grad_reset, grad_update, gated.astype(BF16)], axis=1)
        high, low = split(through + dot_nt(state_back, w_rec))
        grad_high[span, :] = high
        grad_low[span, :] = low
        high, low = split(dot_nt(input_back, w_back))
        return high, low, grad_keyneg

    done = [one_part(part) for part in range(parts)]
    grads = jnp.concatenate([x[0] for x in done] + [x[1] for x in done], axis=0)
    grads_neg = jnp.concatenate([x[2] for x in done], axis=0)
    for first in range(table_rows // 256):
        span = pl.ds(first * 256, 256)
        left = one_hot_rows(rows[16:17, :], rows[24:25, :], 256, first)
        acc[span, :] = dot(jnp.concatenate([left, left], axis=1), grads)
        acc_neg[span, :] = dot(one_hot_rows(rows[32:33, :], rows[40:41, :], 256, first), grads_neg)
        if first == 0:
            for copy in writes:
                copy.start()
    high, low = split(acc_neg[...])
    both = jnp.concatenate([high, low], axis=1)
    total = acc[...] + dot_nt(both, jnp.concatenate([pair, pair], axis=1))
    table_grad[...] = total.astype(BF16)
    for copy in writes:
        copy.wait()


def hold_kernel(source, out):
    out[...] = source[...]


def source_scatter_kernel(rows, grad_high, grad_low, out):
    count = out.shape[0]
    selector = one_hot_rows(rows[0:1, :], rows[8:9, :], count, pl.program_id(0) * (count // 256))
    out[...] = dot(jnp.concatenate([selector] * 2, axis=1), jnp.concatenate([grad_high[...], grad_low[...]], axis=0))


def returned_kernel(wanted, returned, state_grad, out):
    groups = wanted.shape[0] // 2
    high, low = wanted[0:groups, :], wanted[groups:, :]
    count = out.shape[0]
    start = pl.program_id(0) * (count // 256)
    pieces = [one_hot_rows(high[g : g + 1, :], low[g : g + 1, :], count, start) for g in range(high.shape[0])]
    selector = jnp.concatenate(pieces, axis=1)
    out[...] = (state_grad[...] + dot(selector, returned[...])).astype(BF16)


def local(
    memory,
    event_feat,
    event_source,
    event_partner,
    event_negative,
    event_time,
    event_count,
    requests,
    w_input,
    w_state,
    w_pair,
    gate_bias,
    time_freq,
):
    nodes = lax.axis_size("node")
    peers = lax.axis_size("event")
    shards = nodes * peers
    group_rows, width = memory.shape
    _, groups, per_group = requests.shape
    table_rows = groups * per_group
    slots, feat_width = event_feat.shape[2:]
    events = shards * slots

    w_input, w_state, w_pair, gate_bias, time_freq, memory = map(in_hbm, (w_input, w_state, w_pair, gate_bias, time_freq.reshape(1, -1), memory))
    flat = [x[0].T for x in (event_source, event_partner, event_negative, event_time)]
    args = (event_feat[0], *flat, event_count, requests[0])
    message = call(
        functools.partial(pack_kernel, group_rows, table_rows),
        jax.ShapeDtypeStruct((shards, slots + 8, feat_width), BF16),
        args,
        in_specs=[whole(x.shape) for x in args],
        out_specs=whole((shards, slots + 8, feat_width)),
        moved=2 * events * feat_width * 2,
        name="pack",
        vmem=64,
    )
    held = call(
        hold_kernel,
        pltpu.VMEM(memory.shape, BF16),
        (memory,),
        in_specs=[whole(memory.shape)],
        out_specs=whole(memory.shape),
        moved=8 * group_rows * width,
        name="hold",
    )
    message = lax.all_to_all(message, ("node", "event"), 0, 0, tiled=True)
    place = lax.axis_index("event").astype(jnp.int32).reshape(1)
    by_peer = message.reshape(nodes, peers, slots + 8, feat_width)
    tail_spec = pl.BlockSpec((nodes, 1, 8, feat_width), lambda i, at: (0, at[0], slots // 8, 0))
    fetched, wanted = call(
        fetch_kernel,
        (jax.ShapeDtypeStruct((table_rows, width), BF16), jax.ShapeDtypeStruct((2 * groups, per_group), BF16)),
        (place, by_peer, held),
        in_specs=[tail_spec, whole(memory.shape)],
        out_specs=(whole((table_rows, width)), whole((2 * groups, per_group))),
        flops=2 * table_rows * group_rows * width,
        moved=group_rows * width * 2,
        name="fetch",
        prefetch=1,
    )
    table = lax.all_to_all(fetched.reshape(groups, per_group, width), "node", 0, 0, tiled=True).reshape(table_rows, width)

    block = 1024
    turns = events // block
    rows_block = lambda i: (i, 0)
    current, timing, rows = call(
        source_kernel,
        (
            pltpu.HBM((events, width), BF16),
            jax.ShapeDtypeStruct((events, feat_width), BF16),
            jax.ShapeDtypeStruct((48, events), BF16),
        ),
        (message, held, time_freq),
        grid=(turns,),
        in_specs=[
            pl.BlockSpec((block // slots, 8, feat_width), lambda i: (i, slots // 8, 0)),
            whole(memory.shape),
            whole((1, feat_width)),
        ],
        out_specs=(
            pl.BlockSpec((block, width), rows_block),
            pl.BlockSpec((block, feat_width), rows_block),
            pl.BlockSpec((48, block), lambda i: (0, i)),
        ),
        flops=2 * events * group_rows * width,
        moved=4 * events * width,
        trans=events * feat_width,
        name="source",
    )
    in_place = pl.BlockSpec(memory_space=pltpu.HBM)
    table_grad, grad_high, grad_low = call(
        functools.partial(step_kernel, STEP_PARTS),
        (
            jax.ShapeDtypeStruct((table_rows, width), BF16),
            pltpu.HBM((events, width), BF16),
            pltpu.HBM((events, width), BF16),
        ),
        (message, table, timing, rows, gate_bias, in_hbm(current), w_input, w_state, w_pair),
        in_specs=[whole(x.shape) for x in (message, table, timing, rows, gate_bias)] + [in_place] * 4,
        out_specs=(whole((table_rows, width)), in_place, in_place),
        scratch=[
            pltpu.VMEM((table_rows, width), F32),
            pltpu.VMEM((table_rows, width), F32),
            pltpu.VMEM((events, width), BF16),
            pltpu.VMEM(w_input.shape, BF16),
            pltpu.VMEM(w_state.shape, BF16),
            pltpu.VMEM(w_pair.shape, BF16),
            pltpu.VMEM((events, width), BF16),
            pltpu.VMEM((events, width), BF16),
            pltpu.SemaphoreType.DMA((6,)),
        ],
        flops=2 * events * width * (5 * table_rows + 3 * 4 * width + 3 * 3 * width),
        moved=8 * events * width,
        trans=events * width * 3,
        name="step",
    )
    returned = lax.all_to_all(table_grad.reshape(groups, per_group, width), "node", 0, 0, tiled=True).reshape(table_rows, width)
    node_block = 1024
    state_grad = call(
        source_scatter_kernel,
        jax.ShapeDtypeStruct((group_rows, width), F32),
        (rows, in_hbm(grad_high), in_hbm(grad_low)),
        grid=(group_rows // node_block,),
        in_specs=[whole((16, events)), whole(grad_high.shape), whole(grad_low.shape)],
        out_specs=pl.BlockSpec((node_block, width), rows_block),
        flops=4 * events * group_rows * width,
        moved=8 * events * width,
        name="scatter",
    )
    node_block = 1024
    total = call(
        returned_kernel,
        jax.ShapeDtypeStruct((group_rows, width), BF16),
        (wanted, returned, state_grad),
        grid=(group_rows // node_block,),
        in_specs=[whole(wanted.shape), whole((table_rows, width)), pl.BlockSpec((node_block, width), rows_block)],
        out_specs=pl.BlockSpec((node_block, width), rows_block),
        flops=2 * table_rows * group_rows * width,
        moved=6 * group_rows * width,
        name="returned",
    )
    shares = lax.all_to_all(total.reshape(peers, group_rows // peers, width), "event", 0, 0, tiled=True)
    return jnp.sum(shares.astype(F32), axis=0)


def solution(mesh):
    in_specs = (
        P("node", None),
        P(("node", "event"), None, None, None),
        P(("node", "event"), None, None),
        P(("node", "event"), None, None),
        P(("node", "event"), None, None),
        P(("node", "event"), None, None),
        P(("node", "event"), None),
        P(("node", "event"), None, None),
        P(),
        P(),
        P(),
        P(),
        P(),
    )
    out_specs = P(("node", "event"), None)
    return jax.shard_map(local, mesh=mesh, in_specs=in_specs, out_specs=out_specs, check_vma=False)
```

```python
import functools
import math

import jax
import jax.numpy as jnp
from jax import lax
from jax.experimental import pallas as pl
from jax.experimental.pallas import tpu as pltpu
from jax.sharding import PartitionSpec as P

F32 = jnp.float32
BF16 = jnp.bfloat16
STEP_PARTS = 4
AHEAD = 2
PI_HIGH = 3.140625
PI_LOW = math.pi - PI_HIGH


def dot(a, b):
    return jnp.dot(a, b, preferred_element_type=F32)


def dot_nt(a, b):
    return lax.dot_general(a, b, (((1,), (1,)), ((), ())), preferred_element_type=F32)


def iota(shape, dim):
    return lax.broadcasted_iota(jnp.int32, shape, dim)


def split(x):
    high = x.astype(BF16)
    low = (x - high.astype(F32)).astype(BF16)
    return high, low


def call(kernel, outs, args, grid=None, in_specs=None, out_specs=None, scratch=(), flops=0, moved=0, trans=0, name=None, prefetch=0, vmem=48, flags=None):
    spec = pltpu.PrefetchScalarGridSpec(
        num_scalar_prefetch=prefetch,
        grid=grid or (1,),
        in_specs=in_specs,
        out_specs=out_specs,
        scratch_shapes=list(scratch),
    )
    return pl.pallas_call(
        kernel,
        out_shape=outs,
        grid_spec=spec,
        name=name,
        compiler_params=pltpu.CompilerParams(vmem_limit_bytes=min(vmem << 20, 67043328), flags=flags),
        cost_estimate=pl.CostEstimate(flops=int(flops), bytes_accessed=int(moved), transcendentals=int(trans)),
    )(*args)


def in_hbm(x):
    return pltpu.with_memory_space_constraint(x, pltpu.HBM)


def whole(shape):
    return pl.BlockSpec(shape, lambda *_: (0,) * len(shape))


def pack_kernel(group_rows, table_rows, feat, source, partner, negative, time, count, wanted, out):
    shards, slots, width = feat.shape
    groups = wanted.shape[0]
    live = iota((slots, shards), 0) < count[...]
    fields = (
        jnp.where(live, source[...], group_rows),
        jnp.where(live, partner[...], table_rows),
        jnp.where(live, negative[...], table_rows),
        time[...],
    )
    parts = []
    for field in fields:
        parts += [(field >> 8).astype(F32), (field & 255).astype(F32)]
    ids = jnp.concatenate(parts, axis=0).T
    rows = (shards, 8, width)

    def spread(x):
        return jnp.broadcast_to(x[:, None, :], rows)

    def by_group(x):
        return jnp.broadcast_to(x[:, None, :], (groups, shards // groups, width)).reshape(shards, width)

    place = iota(rows, 1)
    high = by_group((wanted[...] >> 8).astype(F32))
    low = by_group((wanted[...] & 255).astype(F32))
    tail = jnp.where(place == 0, spread(ids), jnp.where(place == 1, spread(high), spread(low)))
    out[:, 0:slots, :] = feat[...]
    out[:, slots : slots + 8, :] = tail.astype(BF16)


def field_events(tail):
    blocks = tail.shape[0]
    row = tail[...].astype(F32)[:, 0:1, :]
    shape = (blocks * 16, 128)
    spread = jnp.broadcast_to(row, (blocks, 16, 128)).reshape(shape)
    return jnp.where((iota(shape, 1) & 15) == (iota(shape, 0) & 15), spread, 0.0).astype(BF16)


def columns_of(masked, field):
    lane = iota((128, 256), 0) >> 4
    part = iota((128, 256), 1) >> 7
    weight = jnp.where(lane == 2 * field + part, 1.0, 0.0).astype(BF16)
    both = dot(masked, weight).astype(BF16)
    return both[:, :128], both[:, 128:]


def rows_of(masked, fields):
    shape = (16 * fields, 128)
    weight = jnp.where(iota(shape, 1) >> 4 == iota(shape, 0) >> 3, 1.0, 0.0).astype(BF16)
    return dot_nt(weight, masked).astype(BF16)


def one_hot_columns(high, low, count):
    rows = low.shape[0]
    one, zero, none = (jnp.full((rows, 128), x, BF16) for x in (1.0, 0.0, -1.0))
    lanes = [(iota((rows, 128), 1) + 128 * t).astype(F32).astype(BF16) for t in range(2)]
    pieces = []
    for block in range(count // 256):
        key = jnp.where(high == jnp.full((rows, 128), block, BF16), low, none)
        pieces += [jnp.where(lane == key, one, zero) for lane in lanes]
    return jnp.concatenate(pieces, axis=1)


def one_hot_rows(high, low, count, start=0):
    events = low.shape[1]
    shape = (256, events)
    one, zero = jnp.full(shape, 1.0, BF16), jnp.full(shape, 0.0, BF16)
    place = iota(shape, 0).astype(F32).astype(BF16)
    pieces = []
    for block in range(count // 256):
        number = jnp.asarray(start + block, jnp.int32).astype(F32).astype(BF16)
        key = jnp.where(high == jnp.full((1, events), number, BF16), low, jnp.full((1, events), -1.0, BF16))
        pieces.append(jnp.where(place == jnp.broadcast_to(key, shape), one, zero))
    return jnp.concatenate(pieces, axis=0)


def wanted_values(tail):
    rows = tail[...].astype(F32)[:, 0]
    return rows[:, 1], rows[:, 2]


def fetch_kernel(place, tail, memory, out, wanted):
    high, low = wanted_values(tail)
    wanted[...] = jnp.concatenate([high, low], axis=0).astype(BF16)
    groups = high.shape[0]
    shape = (groups * 128, 128)
    here = iota(shape, 1) == (iota(shape, 0) & 127)

    def spread(x):
        wide = jnp.broadcast_to(x[:, None, :], (groups, 128, 128)).reshape(shape)
        return jnp.where(here, wide, 0.0).astype(BF16)

    ones = jnp.full((128, 128), 1.0, BF16)
    high, low = (dot(spread(x), ones).astype(BF16) for x in (high, low))
    selector = one_hot_columns(high, low, memory.shape[0])
    out[...] = dot(selector, memory[...]).astype(BF16)


def cosine(x):
    turns = jnp.floor(x * (0.5 / math.pi) + 0.5)
    rest = x * 0.5 - turns * PI_HIGH
    rest = rest - turns * PI_LOW
    square = rest * rest
    series = jnp.full_like(x, 1.0 / math.factorial(13))
    for power in (11, 9, 7, 5, 3, 1):
        series = series * square + (-1.0) ** (power // 2) / math.factorial(power)
    sine = series * rest
    return 1.0 - 2.0 * (sine * sine)


def source_kernel(tail, memory, freq, current, timing, rows, cols):
    masked = field_events(tail)
    group = iota((128, 128), 0) >> 4
    weight = jnp.where(group == iota((128, 128), 1) + 2, 1.0, 0.0).astype(BF16)
    cols[...] = dot(masked, weight).astype(BF16)
    rows[...] = rows_of(masked, rows.shape[0] // 16)
    selector = one_hot_columns(*columns_of(masked, 0), memory.shape[0])
    current[...] = dot(selector, memory[...]).astype(BF16)
    high, low = columns_of(masked, 3)
    timing[...] = cosine((high.astype(F32) * 256.0 + low.astype(F32)) * freq[...]).astype(BF16)


def step_kernel(
    parts,
    message,
    table,
    cols,
    rows,
    bias,
    timing_hbm,
    current_hbm,
    w_input_hbm,
    w_state_hbm,
    w_pair_hbm,
    table_grad,
    grad_high_hbm,
    grad_low_hbm,
    acc,
    acc_neg,
    timing,
    current_ref,
    w_input,
    w_state,
    w_pair,
    grad_high,
    grad_low,
    sems,
):
    table_rows, width = table.shape
    blocks = message.shape[0] // parts
    events = blocks * 16
    factor = 1.0 / width**0.5
    reads = [
        pltpu.make_async_copy(a, b, sems.at[i])
        for i, (a, b) in enumerate(
            ((w_input_hbm, w_input), (w_state_hbm, w_state), (w_pair_hbm, w_pair), (current_hbm, current_ref), (timing_hbm, timing))
        )
    ]
    writes = [
        pltpu.make_async_copy(a, b, sems.at[len(reads) + i])
        for i, (a, b) in enumerate(((grad_high, grad_high_hbm), (grad_low, grad_low_hbm)))
    ]
    for copy in reads:
        copy.start()

    def rows_for(part):
        mine = message[part * blocks : (part + 1) * blocks]
        ids = cols[pl.ds(part * events, events), :].astype(F32)
        spread = [jnp.broadcast_to(ids[:, i : i + 1], ids.shape).astype(BF16) for i in range(4)]
        partner = dot(one_hot_columns(spread[0], spread[1], table_rows), table[...]).astype(BF16)
        negative = dot(one_hot_columns(spread[2], spread[3], table_rows), table[...]).astype(BF16)
        return mine[:, 0:16, :].reshape(events, 128), partner, negative

    first_rows = [rows_for(part) for part in range(AHEAD)]
    for copy in reads:
        copy.wait()
    w_in, w_rec, pair = w_input[...], w_state[...], w_pair[...]
    w_gates = jnp.concatenate([w_in[:, : 2 * width], w_rec[:, : 2 * width]], axis=0)
    w_back = jnp.concatenate([w_in[:width, :], pair], axis=1)
    gate = bias[...].reshape(1, -1)

    def one_part(part):
        span = pl.ds(part * events, events)
        feature, partner, negative = first_rows[part] if part < AHEAD else rows_for(part)
        current = current_ref[span, :]
        joined = jnp.concatenate([partner, feature, timing[span, :]], axis=1)
        gates = dot(jnp.concatenate([joined, current], axis=1), w_gates) + gate[:, : 2 * width]
        reset = jax.nn.sigmoid(gates[:, :width])
        update = jax.nn.sigmoid(gates[:, width:])
        recurrent = dot(current, w_rec[:, 2 * width :])
        candidate = jnp.tanh(dot(joined, w_in[:, 2 * width :]) + gate[:, 2 * width :] + reset * recurrent)
        change = current.astype(F32) - candidate
        renewed = candidate + update * change
        key_pos = dot(partner, pair)
        key_neg = dot(negative, pair)
        score_pos = jnp.sum(renewed * key_pos, axis=1, keepdims=True) * factor
        score_neg = jnp.sum(renewed * key_neg, axis=1, keepdims=True) * factor
        weight_pos = jax.nn.sigmoid(-score_pos) * -factor
        weight_neg = jax.nn.sigmoid(score_neg) * factor
        grad_renewed = weight_pos * key_pos + weight_neg * key_neg
        grad_keypos = (weight_pos * renewed).astype(BF16)
        grad_keyneg = (weight_neg * renewed).astype(BF16)
        through = grad_renewed * update
        grad_cand = (grad_renewed - through) * (1.0 - candidate * candidate)
        gated = grad_cand * reset
        grad_reset = (gated * recurrent * (1.0 - reset)).astype(BF16)
        grad_update = (through * change * (1.0 - update)).astype(BF16)
        input_back = jnp.concatenate([grad_reset, grad_update, grad_cand.astype(BF16), grad_keypos], axis=1)
        state_back = jnp.concatenate([grad_reset, grad_update, gated.astype(BF16)], axis=1)
        high, low = split(through + dot_nt(state_back, w_rec))
        grad_high[span, :] = high
        grad_low[span, :] = low
        high, low = split(dot_nt(input_back, w_back))
        return high, low, grad_keyneg

    done = [one_part(part) for part in range(parts)]
    grads = jnp.concatenate([x[0] for x in done] + [x[1] for x in done], axis=0)
    grads_neg = jnp.concatenate([x[2] for x in done], axis=0)
    for first in range(table_rows // 256):
        span = pl.ds(first * 256, 256)
        left = one_hot_rows(rows[16:17, :], rows[24:25, :], 256, first)
        acc[span, :] = dot(jnp.concatenate([left, left], axis=1), grads)
        acc_neg[span, :] = dot(one_hot_rows(rows[32:33, :], rows[40:41, :], 256, first), grads_neg)
    for copy in writes:
        copy.start()
    high, low = split(acc_neg[...])
    both = jnp.concatenate([high, low], axis=1)
    total = acc[...] + dot_nt(both, jnp.concatenate([pair, pair], axis=1))
    table_grad[...] = total.astype(BF16)
    for copy in writes:
        copy.wait()


def hold_kernel(source, out):
    out[...] = source[...]


def source_scatter_kernel(rows, grad_high, grad_low, out):
    count = out.shape[0]
    selector = one_hot_rows(rows[0:1, :], rows[8:9, :], count, pl.program_id(0) * (count // 256))
    out[...] = dot(jnp.concatenate([selector] * 2, axis=1), jnp.concatenate([grad_high[...], grad_low[...]], axis=0))


def returned_kernel(wanted, returned, state_grad, out):
    groups = wanted.shape[0] // 2
    high, low = wanted[0:groups, :], wanted[groups:, :]
    count = out.shape[0]
    start = pl.program_id(0) * (count // 256)
    pieces = [one_hot_rows(high[g : g + 1, :], low[g : g + 1, :], count, start) for g in range(high.shape[0])]
    selector = jnp.concatenate(pieces, axis=1)
    out[...] = (state_grad[...] + dot(selector, returned[...])).astype(BF16)


def step_call(message, table, cols, rows, gate_bias, timing, current, w_input, w_state, w_pair):
    table_rows, width = table.shape
    events = current.shape[0]
    in_place = pl.BlockSpec(memory_space=pltpu.HBM)
    return call(
        functools.partial(step_kernel, STEP_PARTS),
        (
            jax.ShapeDtypeStruct((table_rows, width), BF16),
            pltpu.HBM((events, width), BF16),
            pltpu.HBM((events, width), BF16),
        ),
        (message, table, cols, rows, gate_bias, timing, current, w_input, w_state, w_pair),
        in_specs=[whole(x.shape) for x in (message, table, cols, rows, gate_bias)] + [in_place] * 5,
        out_specs=(whole((table_rows, width)), in_place, in_place),
        scratch=[
            pltpu.VMEM((table_rows, width), F32),
            pltpu.VMEM((table_rows, width), F32),
            pltpu.VMEM(timing.shape, BF16),
            pltpu.VMEM((events, width), BF16),
            pltpu.VMEM(w_input.shape, BF16),
            pltpu.VMEM(w_state.shape, BF16),
            pltpu.VMEM(w_pair.shape, BF16),
            pltpu.VMEM((events, width), BF16),
            pltpu.VMEM((events, width), BF16),
            pltpu.SemaphoreType.DMA((7,)),
        ],
        flops=2 * events * width * (5 * table_rows + 3 * 4 * width + 3 * 3 * width),
        moved=8 * events * width,
        trans=events * width * 3,
        name="step",
    )


def local(
    memory,
    event_feat,
    event_source,
    event_partner,
    event_negative,
    event_time,
    event_count,
    requests,
    w_input,
    w_state,
    w_pair,
    gate_bias,
    time_freq,
):
    nodes = lax.axis_size("node")
    peers = lax.axis_size("event")
    shards = nodes * peers
    group_rows, width = memory.shape
    _, groups, per_group = requests.shape
    table_rows = groups * per_group
    slots, feat_width = event_feat.shape[2:]
    events = shards * slots

    w_input, w_state, w_pair, gate_bias, time_freq, memory = map(in_hbm, (w_input, w_state, w_pair, gate_bias, time_freq.reshape(1, -1), memory))
    flat = [x[0].T for x in (event_source, event_partner, event_negative, event_time)]
    args = (event_feat[0], *flat, event_count, requests[0])
    message = call(
        functools.partial(pack_kernel, group_rows, table_rows),
        jax.ShapeDtypeStruct((shards, slots + 8, feat_width), BF16),
        args,
        in_specs=[whole(x.shape) for x in args],
        out_specs=whole((shards, slots + 8, feat_width)),
        moved=2 * events * feat_width * 2,
        name="pack",
        vmem=64,
    )
    held = call(
        hold_kernel,
        pltpu.VMEM(memory.shape, BF16),
        (memory,),
        in_specs=[whole(memory.shape)],
        out_specs=whole(memory.shape),
        moved=8 * group_rows * width,
        name="hold",
    )
    message = lax.all_to_all(message, ("node", "event"), 0, 0, tiled=True)
    place = lax.axis_index("event").astype(jnp.int32).reshape(1)
    by_peer = message.reshape(nodes, peers, slots + 8, feat_width)
    tail_spec = pl.BlockSpec((nodes, 1, 8, feat_width), lambda i, at: (0, at[0], slots // 8, 0))
    fetched, wanted = call(
        fetch_kernel,
        (jax.ShapeDtypeStruct((table_rows, width), BF16), jax.ShapeDtypeStruct((2 * groups, per_group), BF16)),
        (place, by_peer, held),
        in_specs=[tail_spec, whole(memory.shape)],
        out_specs=(whole((table_rows, width)), whole((2 * groups, per_group))),
        flops=2 * table_rows * group_rows * width,
        moved=group_rows * width * 2,
        name="fetch",
        prefetch=1,
    )
    table = lax.all_to_all(fetched.reshape(groups, per_group, width), "node", 0, 0, tiled=True).reshape(table_rows, width)

    block = 1024
    turns = events // block
    rows_block = lambda i: (i, 0)
    current, timing, rows, cols = call(
        source_kernel,
        (
            pltpu.HBM((events, width), BF16),
            pltpu.HBM((events, feat_width), BF16),
            jax.ShapeDtypeStruct((48, events), BF16),
            jax.ShapeDtypeStruct((events, feat_width), BF16),
        ),
        (message, held, time_freq),
        grid=(turns,),
        in_specs=[
            pl.BlockSpec((block // slots, 8, feat_width), lambda i: (i, slots // 8, 0)),
            whole(memory.shape),
            whole((1, feat_width)),
        ],
        out_specs=(
            pl.BlockSpec((block, width), rows_block),
            pl.BlockSpec((block, feat_width), rows_block),
            pl.BlockSpec((48, block), lambda i: (0, i)),
            pl.BlockSpec((block, feat_width), rows_block),
        ),
        flops=2 * events * group_rows * width,
        moved=4 * events * width,
        trans=events * feat_width,
        name="source",
    )
    table_grad, grad_high, grad_low = step_call(
        message, table, cols, rows, gate_bias, in_hbm(timing), in_hbm(current), w_input, w_state, w_pair
    )
    returned = lax.all_to_all(table_grad.reshape(groups, per_group, width), "node", 0, 0, tiled=True).reshape(table_rows, width)
    node_block = 1024
    state_grad = call(
        source_scatter_kernel,
        jax.ShapeDtypeStruct((group_rows, width), F32),
        (rows, in_hbm(grad_high), in_hbm(grad_low)),
        grid=(group_rows // node_block,),
        in_specs=[whole((16, events)), whole(grad_high.shape), whole(grad_low.shape)],
        out_specs=pl.BlockSpec((node_block, width), rows_block),
        flops=4 * events * group_rows * width,
        moved=8 * events * width,
        name="scatter",
    )
    node_block = 1024
    total = call(
        returned_kernel,
        jax.ShapeDtypeStruct((group_rows, width), BF16),
        (wanted, returned, state_grad),
        grid=(group_rows // node_block,),
        in_specs=[whole(wanted.shape), whole((table_rows, width)), pl.BlockSpec((node_block, width), rows_block)],
        out_specs=pl.BlockSpec((node_block, width), rows_block),
        flops=2 * table_rows * group_rows * width,
        moved=6 * group_rows * width,
        name="returned",
    )
    shares = lax.all_to_all(total.reshape(peers, group_rows // peers, width), "event", 0, 0, tiled=True)
    return jnp.sum(shares.astype(F32), axis=0)


def solution(mesh):
    in_specs = (
        P("node", None),
        P(("node", "event"), None, None, None),
        P(("node", "event"), None, None),
        P(("node", "event"), None, None),
        P(("node", "event"), None, None),
        P(("node", "event"), None, None),
        P(("node", "event"), None),
        P(("node", "event"), None, None),
        P(),
        P(),
        P(),
        P(),
        P(),
    )
    out_specs = P(("node", "event"), None)
    return jax.shard_map(local, mesh=mesh, in_specs=in_specs, out_specs=out_specs, check_vma=False)
```

```python
import functools
import math

import jax
import jax.numpy as jnp
from jax import lax
from jax.experimental import pallas as pl
from jax.experimental.pallas import tpu as pltpu
from jax.sharding import PartitionSpec as P

F32 = jnp.float32
BF16 = jnp.bfloat16
STEP_PARTS = 4
PACK_CHUNKS = 4
AHEAD = 2
PI_HIGH = 3.140625
PI_LOW = math.pi - PI_HIGH


def dot(a, b):
    return jnp.dot(a, b, preferred_element_type=F32)


def dot_nt(a, b):
    return lax.dot_general(a, b, (((1,), (1,)), ((), ())), preferred_element_type=F32)


def iota(shape, dim):
    return lax.broadcasted_iota(jnp.int32, shape, dim)


def split(x):
    high = x.astype(BF16)
    low = (x - high.astype(F32)).astype(BF16)
    return high, low


def call(kernel, outs, args, grid=None, in_specs=None, out_specs=None, scratch=(), flops=0, moved=0, trans=0, name=None, prefetch=0, vmem=48, flags=None):
    spec = pltpu.PrefetchScalarGridSpec(
        num_scalar_prefetch=prefetch,
        grid=grid or (1,),
        in_specs=in_specs,
        out_specs=out_specs,
        scratch_shapes=list(scratch),
    )
    return pl.pallas_call(
        kernel,
        out_shape=outs,
        grid_spec=spec,
        name=name,
        compiler_params=pltpu.CompilerParams(vmem_limit_bytes=min(vmem << 20, 67043328), flags=flags),
        cost_estimate=pl.CostEstimate(flops=int(flops), bytes_accessed=int(moved), transcendentals=int(trans)),
    )(*args)


def in_hbm(x):
    return pltpu.with_memory_space_constraint(x, pltpu.HBM)


def whole(shape):
    return pl.BlockSpec(shape, lambda *_: (0,) * len(shape))


def pack_kernel(group_rows, table_rows, *refs):
    feat, *small_hbm, out, buf, source, partner, negative, time, count, wanted, sems = refs
    small = (source, partner, negative, time, count, wanted)
    shards, slots, width = feat.shape
    groups = wanted.shape[0]
    chunk = shards // PACK_CHUNKS
    reads = [pltpu.make_async_copy(a, b, sems.at[i]) for i, (a, b) in enumerate(zip(small_hbm, small))]
    spans = [pl.ds(chunk * i, chunk) for i in range(PACK_CHUNKS)]
    features = [
        pltpu.make_async_copy(feat.at[span], buf.at[span, 0:slots], sems.at[len(small) + i]) for i, span in enumerate(spans)
    ]
    writes = [
        pltpu.make_async_copy(buf.at[span], out.at[span], sems.at[len(small) + PACK_CHUNKS + i])
        for i, span in enumerate(spans)
    ]
    for copy in reads + features:
        copy.start()
    for copy in reads:
        copy.wait()
    live = iota((slots, shards), 0) < count[...]
    fields = (
        jnp.where(live, source[...], group_rows),
        jnp.where(live, partner[...], table_rows),
        jnp.where(live, negative[...], table_rows),
        time[...],
    )
    parts = []
    for field in fields:
        parts += [(field >> 8).astype(F32), (field & 255).astype(F32)]
    ids = jnp.concatenate(parts, axis=0).T
    rows = (shards, 8, width)

    def spread(x):
        return jnp.broadcast_to(x[:, None, :], rows)

    def by_group(x):
        return jnp.broadcast_to(x[:, None, :], (groups, shards // groups, width)).reshape(shards, width)

    place = iota(rows, 1)
    high = by_group((wanted[...] >> 8).astype(F32))
    low = by_group((wanted[...] & 255).astype(F32))
    tail = jnp.where(place == 0, spread(ids), jnp.where(place == 1, spread(high), spread(low)))
    buf[:, slots : slots + 8, :] = tail.astype(BF16)
    for read, write in zip(features, writes):
        read.wait()
        write.start()
    for write in writes:
        write.wait()


def field_events(tail):
    blocks = tail.shape[0]
    row = tail[...].astype(F32)[:, 0:1, :]
    shape = (blocks * 16, 128)
    spread = jnp.broadcast_to(row, (blocks, 16, 128)).reshape(shape)
    return jnp.where((iota(shape, 1) & 15) == (iota(shape, 0) & 15), spread, 0.0).astype(BF16)


def columns_of(masked, field):
    lane = iota((128, 256), 0) >> 4
    part = iota((128, 256), 1) >> 7
    weight = jnp.where(lane == 2 * field + part, 1.0, 0.0).astype(BF16)
    both = dot(masked, weight).astype(BF16)
    return both[:, :128], both[:, 128:]


def rows_of(masked, fields):
    shape = (16 * fields, 128)
    weight = jnp.where(iota(shape, 1) >> 4 == iota(shape, 0) >> 3, 1.0, 0.0).astype(BF16)
    return dot_nt(weight, masked).astype(BF16)


def one_hot_columns(high, low, count):
    rows = low.shape[0]
    one, zero, none = (jnp.full((rows, 128), x, BF16) for x in (1.0, 0.0, -1.0))
    lanes = [(iota((rows, 128), 1) + 128 * t).astype(F32).astype(BF16) for t in range(2)]
    pieces = []
    for block in range(count // 256):
        key = jnp.where(high == jnp.full((rows, 128), block, BF16), low, none)
        pieces += [jnp.where(lane == key, one, zero) for lane in lanes]
    return jnp.concatenate(pieces, axis=1)


def one_hot_rows(high, low, count, start=0):
    events = low.shape[1]
    shape = (256, events)
    one, zero = jnp.full(shape, 1.0, BF16), jnp.full(shape, 0.0, BF16)
    place = iota(shape, 0).astype(F32).astype(BF16)
    pieces = []
    for block in range(count // 256):
        number = jnp.asarray(start + block, jnp.int32).astype(F32).astype(BF16)
        key = jnp.where(high == jnp.full((1, events), number, BF16), low, jnp.full((1, events), -1.0, BF16))
        pieces.append(jnp.where(place == jnp.broadcast_to(key, shape), one, zero))
    return jnp.concatenate(pieces, axis=0)


def wanted_values(tail):
    rows = tail[...].astype(F32)[:, 0]
    return rows[:, 1], rows[:, 2]


def fetch_kernel(place, tail, memory, out, wanted):
    high, low = wanted_values(tail)
    wanted[...] = jnp.concatenate([high, low], axis=0).astype(BF16)
    groups = high.shape[0]
    shape = (groups * 128, 128)
    here = iota(shape, 1) == (iota(shape, 0) & 127)

    def spread(x):
        wide = jnp.broadcast_to(x[:, None, :], (groups, 128, 128)).reshape(shape)
        return jnp.where(here, wide, 0.0).astype(BF16)

    ones = jnp.full((128, 128), 1.0, BF16)
    high, low = (dot(spread(x), ones).astype(BF16) for x in (high, low))
    selector = one_hot_columns(high, low, memory.shape[0])
    out[...] = dot(selector, memory[...]).astype(BF16)


def cosine(x):
    turns = jnp.floor(x * (0.5 / math.pi) + 0.5)
    rest = x * 0.5 - turns * PI_HIGH
    rest = rest - turns * PI_LOW
    square = rest * rest
    series = jnp.full_like(x, 1.0 / math.factorial(13))
    for power in (11, 9, 7, 5, 3, 1):
        series = series * square + (-1.0) ** (power // 2) / math.factorial(power)
    sine = series * rest
    return 1.0 - 2.0 * (sine * sine)


def source_kernel(tail, memory, freq, current, timing, rows, cols):
    masked = field_events(tail)
    group = iota((128, 128), 0) >> 4
    weight = jnp.where(group == iota((128, 128), 1) + 2, 1.0, 0.0).astype(BF16)
    cols[...] = dot(masked, weight).astype(BF16)
    rows[...] = rows_of(masked, rows.shape[0] // 16)
    selector = one_hot_columns(*columns_of(masked, 0), memory.shape[0])
    current[...] = dot(selector, memory[...]).astype(BF16)
    high, low = columns_of(masked, 3)
    timing[...] = cosine((high.astype(F32) * 256.0 + low.astype(F32)) * freq[...]).astype(BF16)


def step_kernel(
    parts,
    message,
    table,
    cols,
    rows,
    bias,
    timing_hbm,
    current_hbm,
    w_input_hbm,
    w_state_hbm,
    w_pair_hbm,
    table_grad,
    grad_high_hbm,
    grad_low_hbm,
    acc,
    acc_neg,
    timing,
    current_ref,
    w_input,
    w_state,
    w_pair,
    grad_high,
    grad_low,
    sems,
):
    table_rows, width = table.shape
    blocks = message.shape[0] // parts
    events = blocks * 16
    factor = 1.0 / width**0.5
    reads = [
        pltpu.make_async_copy(a, b, sems.at[i])
        for i, (a, b) in enumerate(
            ((w_input_hbm, w_input), (w_state_hbm, w_state), (w_pair_hbm, w_pair), (current_hbm, current_ref), (timing_hbm, timing))
        )
    ]
    writes = [
        pltpu.make_async_copy(a, b, sems.at[len(reads) + i])
        for i, (a, b) in enumerate(((grad_high, grad_high_hbm), (grad_low, grad_low_hbm)))
    ]
    for copy in reads:
        copy.start()

    def rows_for(part):
        mine = message[part * blocks : (part + 1) * blocks]
        ids = cols[pl.ds(part * events, events), :].astype(F32)
        spread = [jnp.broadcast_to(ids[:, i : i + 1], ids.shape).astype(BF16) for i in range(4)]
        partner = dot(one_hot_columns(spread[0], spread[1], table_rows), table[...]).astype(BF16)
        negative = dot(one_hot_columns(spread[2], spread[3], table_rows), table[...]).astype(BF16)
        return mine[:, 0:16, :].reshape(events, 128), partner, negative

    first_rows = [rows_for(part) for part in range(AHEAD)]
    for copy in reads:
        copy.wait()
    w_in, w_rec, pair = w_input[...], w_state[...], w_pair[...]
    w_gates = jnp.concatenate([w_in[:, : 2 * width], w_rec[:, : 2 * width]], axis=0)
    w_back = jnp.concatenate([w_in[:width, :], pair], axis=1)
    gate = bias[...].reshape(1, -1)

    def one_part(part):
        span = pl.ds(part * events, events)
        feature, partner, negative = first_rows[part] if part < AHEAD else rows_for(part)
        current = current_ref[span, :]
        joined = jnp.concatenate([partner, feature, timing[span, :]], axis=1)
        gates = dot(jnp.concatenate([joined, current], axis=1), w_gates) + gate[:, : 2 * width]
        reset = jax.nn.sigmoid(gates[:, :width])
        update = jax.nn.sigmoid(gates[:, width:])
        recurrent = dot(current, w_rec[:, 2 * width :])
        candidate = jnp.tanh(dot(joined, w_in[:, 2 * width :]) + gate[:, 2 * width :] + reset * recurrent)
        change = current.astype(F32) - candidate
        renewed = candidate + update * change
        key_pos = dot(partner, pair)
        key_neg = dot(negative, pair)
        score_pos = jnp.sum(renewed * key_pos, axis=1, keepdims=True) * factor
        score_neg = jnp.sum(renewed * key_neg, axis=1, keepdims=True) * factor
        weight_pos = jax.nn.sigmoid(-score_pos) * -factor
        weight_neg = jax.nn.sigmoid(score_neg) * factor
        grad_renewed = weight_pos * key_pos + weight_neg * key_neg
        grad_keypos = (weight_pos * renewed).astype(BF16)
        grad_keyneg = (weight_neg * renewed).astype(BF16)
        through = grad_renewed * update
        grad_cand = (grad_renewed - through) * (1.0 - candidate * candidate)
        gated = grad_cand * reset
        grad_reset = (gated * recurrent * (1.0 - reset)).astype(BF16)
        grad_update = (through * change * (1.0 - update)).astype(BF16)
        input_back = jnp.concatenate([grad_reset, grad_update, grad_cand.astype(BF16), grad_keypos], axis=1)
        state_back = jnp.concatenate([grad_reset, grad_update, gated.astype(BF16)], axis=1)
        high, low = split(through + dot_nt(state_back, w_rec))
        grad_high[span, :] = high
        grad_low[span, :] = low
        high, low = split(dot_nt(input_back, w_back))
        return high, low, grad_keyneg

    done = [one_part(part) for part in range(parts)]
    grads = jnp.concatenate([x[0] for x in done] + [x[1] for x in done], axis=0)
    grads_neg = jnp.concatenate([x[2] for x in done], axis=0)
    for first in range(table_rows // 256):
        span = pl.ds(first * 256, 256)
        left = one_hot_rows(rows[16:17, :], rows[24:25, :], 256, first)
        acc[span, :] = dot(jnp.concatenate([left, left], axis=1), grads)
        acc_neg[span, :] = dot(one_hot_rows(rows[32:33, :], rows[40:41, :], 256, first), grads_neg)
    for copy in writes:
        copy.start()
    high, low = split(acc_neg[...])
    both = jnp.concatenate([high, low], axis=1)
    total = acc[...] + dot_nt(both, jnp.concatenate([pair, pair], axis=1))
    table_grad[...] = total.astype(BF16)
    for copy in writes:
        copy.wait()


def hold_kernel(source, out):
    out[...] = source[...]


def source_scatter_kernel(rows, grad_high, grad_low, out):
    count = out.shape[0]
    selector = one_hot_rows(rows[0:1, :], rows[8:9, :], count, pl.program_id(0) * (count // 256))
    out[...] = dot(jnp.concatenate([selector] * 2, axis=1), jnp.concatenate([grad_high[...], grad_low[...]], axis=0))


def returned_kernel(wanted, returned, state_grad, out):
    half = wanted.shape[0] // 4
    high, low = (
        jnp.concatenate([wanted[at : at + half, :], wanted[at + 2 * half : at + 3 * half, :]], axis=0) for at in (0, half)
    )
    count = out.shape[0]
    start = pl.program_id(0) * (count // 256)
    pieces = [one_hot_rows(high[g : g + 1, :], low[g : g + 1, :], count, start) for g in range(high.shape[0])]
    selector = jnp.concatenate(pieces, axis=1)
    out[...] = (state_grad[...] + dot(selector, returned[...])).astype(BF16)


def step_call(message, table, cols, rows, gate_bias, timing, current, w_input, w_state, w_pair):
    table_rows, width = table.shape
    events = current.shape[0]
    in_place = pl.BlockSpec(memory_space=pltpu.HBM)
    return call(
        functools.partial(step_kernel, STEP_PARTS),
        (
            jax.ShapeDtypeStruct((table_rows, width), BF16),
            pltpu.HBM((events, width), BF16),
            pltpu.HBM((events, width), BF16),
        ),
        (message, table, cols, rows, gate_bias, timing, current, w_input, w_state, w_pair),
        in_specs=[whole(x.shape) for x in (message, table, cols, rows, gate_bias)] + [in_place] * 5,
        out_specs=(whole((table_rows, width)), in_place, in_place),
        scratch=[
            pltpu.VMEM((table_rows, width), F32),
            pltpu.VMEM((table_rows, width), F32),
            pltpu.VMEM(timing.shape, BF16),
            pltpu.VMEM((events, width), BF16),
            pltpu.VMEM(w_input.shape, BF16),
            pltpu.VMEM(w_state.shape, BF16),
            pltpu.VMEM(w_pair.shape, BF16),
            pltpu.VMEM((events, width), BF16),
            pltpu.VMEM((events, width), BF16),
            pltpu.SemaphoreType.DMA((7,)),
        ],
        flops=2 * events * width * (5 * table_rows + 3 * 4 * width + 3 * 3 * width),
        moved=8 * events * width,
        trans=events * width * 3,
        name="step",
    )


def local(
    memory,
    event_feat,
    event_source,
    event_partner,
    event_negative,
    event_time,
    event_count,
    requests,
    w_input,
    w_state,
    w_pair,
    gate_bias,
    time_freq,
):
    nodes = lax.axis_size("node")
    peers = lax.axis_size("event")
    shards = nodes * peers
    group_rows, width = memory.shape
    _, groups, per_group = requests.shape
    table_rows = groups * per_group
    slots, feat_width = event_feat.shape[2:]
    events = shards * slots

    w_input, w_state, w_pair, gate_bias, time_freq, memory = map(in_hbm, (w_input, w_state, w_pair, gate_bias, time_freq.reshape(1, -1), memory))
    flat = [x[0].T for x in (event_source, event_partner, event_negative, event_time)]
    args = tuple(map(in_hbm, (event_feat[0], *flat, event_count, requests[0])))
    in_place = pl.BlockSpec(memory_space=pltpu.HBM)
    message = call(
        functools.partial(pack_kernel, group_rows, table_rows),
        pltpu.HBM((shards, slots + 8, feat_width), BF16),
        args,
        in_specs=[in_place] * len(args),
        out_specs=in_place,
        scratch=[
            pltpu.VMEM((shards, slots + 8, feat_width), BF16),
            *(pltpu.VMEM(x.shape, x.dtype) for x in args[1:]),
            pltpu.SemaphoreType.DMA((len(args) - 1 + 2 * PACK_CHUNKS,)),
        ],
        moved=2 * events * feat_width * 2,
        name="pack",
    )
    held = call(
        hold_kernel,
        pltpu.VMEM(memory.shape, BF16),
        (memory,),
        in_specs=[whole(memory.shape)],
        out_specs=whole(memory.shape),
        moved=8 * group_rows * width,
        name="hold",
    )
    message = lax.all_to_all(message, ("node", "event"), 0, 0, tiled=True)
    place = lax.axis_index("event").astype(jnp.int32).reshape(1)
    by_peer = message.reshape(nodes, peers, slots + 8, feat_width)
    tail_spec = pl.BlockSpec((nodes // 2, 1, 8, feat_width), lambda i, at: (i, at[0], slots // 8, 0))
    fetched, wanted = call(
        fetch_kernel,
        (jax.ShapeDtypeStruct((table_rows, width), BF16), jax.ShapeDtypeStruct((2 * groups, per_group), BF16)),
        (place, by_peer, held),
        grid=(2,),
        in_specs=[tail_spec, whole(memory.shape)],
        out_specs=(
            pl.BlockSpec((table_rows // 2, width), lambda i, at: (i, 0)),
            pl.BlockSpec((groups, per_group), lambda i, at: (i, 0)),
        ),
        flops=2 * table_rows * group_rows * width,
        moved=group_rows * width * 2,
        name="fetch",
        prefetch=1,
    )
    table = lax.all_to_all(fetched.reshape(groups, per_group, width), "node", 0, 0, tiled=True).reshape(table_rows, width)

    block = 1024
    turns = events // block
    rows_block = lambda i: (i, 0)
    current, timing, rows, cols = call(
        source_kernel,
        (
            pltpu.HBM((events, width), BF16),
            pltpu.HBM((events, feat_width), BF16),
            jax.ShapeDtypeStruct((48, events), BF16),
            jax.ShapeDtypeStruct((events, feat_width), BF16),
        ),
        (message, held, time_freq),
        grid=(turns,),
        in_specs=[
            pl.BlockSpec((block // slots, 8, feat_width), lambda i: (i, slots // 8, 0)),
            whole(memory.shape),
            whole((1, feat_width)),
        ],
        out_specs=(
            pl.BlockSpec((block, width), rows_block),
            pl.BlockSpec((block, feat_width), rows_block),
            pl.BlockSpec((48, block), lambda i: (0, i)),
            pl.BlockSpec((block, feat_width), rows_block),
        ),
        flops=2 * events * group_rows * width,
        moved=4 * events * width,
        trans=events * feat_width,
        name="source",
    )
    table_grad, grad_high, grad_low = step_call(
        message, table, cols, rows, gate_bias, in_hbm(timing), in_hbm(current), w_input, w_state, w_pair
    )
    returned = lax.all_to_all(table_grad.reshape(groups, per_group, width), "node", 0, 0, tiled=True).reshape(table_rows, width)
    node_block = 1024
    state_grad = call(
        source_scatter_kernel,
        jax.ShapeDtypeStruct((group_rows, width), F32),
        (rows, in_hbm(grad_high), in_hbm(grad_low)),
        grid=(group_rows // node_block,),
        in_specs=[whole((16, events)), whole(grad_high.shape), whole(grad_low.shape)],
        out_specs=pl.BlockSpec((node_block, width), rows_block),
        flops=4 * events * group_rows * width,
        moved=8 * events * width,
        name="scatter",
    )
    node_block = 1024
    total = call(
        returned_kernel,
        jax.ShapeDtypeStruct((group_rows, width), BF16),
        (wanted, returned, state_grad),
        grid=(group_rows // node_block,),
        in_specs=[whole(wanted.shape), whole((table_rows, width)), pl.BlockSpec((node_block, width), rows_block)],
        out_specs=pl.BlockSpec((node_block, width), rows_block),
        flops=2 * table_rows * group_rows * width,
        moved=6 * group_rows * width,
        name="returned",
    )
    shares = lax.all_to_all(total.reshape(peers, group_rows // peers, width), "event", 0, 0, tiled=True)
    return jnp.sum(shares.astype(F32), axis=0)


def solution(mesh):
    in_specs = (
        P("node", None),
        P(("node", "event"), None, None, None),
        P(("node", "event"), None, None),
        P(("node", "event"), None, None),
        P(("node", "event"), None, None),
        P(("node", "event"), None, None),
        P(("node", "event"), None),
        P(("node", "event"), None, None),
        P(),
        P(),
        P(),
        P(),
        P(),
    )
    out_specs = P(("node", "event"), None)
    return jax.shard_map(local, mesh=mesh, in_specs=in_specs, out_specs=out_specs, check_vma=False)
```

```python
import functools
import math

import jax
import jax.numpy as jnp
from jax import lax
from jax.experimental import pallas as pl
from jax.experimental.pallas import tpu as pltpu
from jax.sharding import PartitionSpec as P

F32 = jnp.float32
BF16 = jnp.bfloat16
STEP_PARTS = 4
PACK_CHUNKS = 4
AHEAD = 3
PI_HIGH = 3.140625
PI_LOW = math.pi - PI_HIGH


def dot(a, b):
    return jnp.dot(a, b, preferred_element_type=F32)


def dot_nt(a, b):
    return lax.dot_general(a, b, (((1,), (1,)), ((), ())), preferred_element_type=F32)


def iota(shape, dim):
    return lax.broadcasted_iota(jnp.int32, shape, dim)


def split(x):
    high = x.astype(BF16)
    low = (x - high.astype(F32)).astype(BF16)
    return high, low


def call(kernel, outs, args, grid=None, in_specs=None, out_specs=None, scratch=(), flops=0, moved=0, trans=0, name=None, prefetch=0, vmem=48, flags=None):
    spec = pltpu.PrefetchScalarGridSpec(
        num_scalar_prefetch=prefetch,
        grid=grid or (1,),
        in_specs=in_specs,
        out_specs=out_specs,
        scratch_shapes=list(scratch),
    )
    return pl.pallas_call(
        kernel,
        out_shape=outs,
        grid_spec=spec,
        name=name,
        compiler_params=pltpu.CompilerParams(vmem_limit_bytes=min(vmem << 20, 67043328), flags=flags),
        cost_estimate=pl.CostEstimate(flops=int(flops), bytes_accessed=int(moved), transcendentals=int(trans)),
    )(*args)


def in_hbm(x):
    return pltpu.with_memory_space_constraint(x, pltpu.HBM)


def whole(shape):
    return pl.BlockSpec(shape, lambda *_: (0,) * len(shape))


def pack_kernel(group_rows, table_rows, *refs):
    feat, *small_hbm, out, buf, source, partner, negative, time, count, wanted, sems = refs
    small = (source, partner, negative, time, count, wanted)
    shards, slots, width = feat.shape
    groups = wanted.shape[0]
    chunk = shards // PACK_CHUNKS
    reads = [pltpu.make_async_copy(a, b, sems.at[i]) for i, (a, b) in enumerate(zip(small_hbm, small))]
    spans = [pl.ds(chunk * i, chunk) for i in range(PACK_CHUNKS)]
    features = [
        pltpu.make_async_copy(feat.at[span], buf.at[span, 0:slots], sems.at[len(small) + i]) for i, span in enumerate(spans)
    ]
    writes = [
        pltpu.make_async_copy(buf.at[span], out.at[span], sems.at[len(small) + PACK_CHUNKS + i])
        for i, span in enumerate(spans)
    ]
    for copy in reads + features:
        copy.start()
    for copy in reads:
        copy.wait()
    live = iota((slots, shards), 0) < count[...]
    fields = (
        jnp.where(live, source[...], group_rows),
        jnp.where(live, partner[...], table_rows),
        jnp.where(live, negative[...], table_rows),
        time[...],
    )
    parts = []
    for field in fields:
        parts += [(field >> 8).astype(F32), (field & 255).astype(F32)]
    ids = jnp.concatenate(parts, axis=0).T
    rows = (shards, 8, width)

    def spread(x):
        return jnp.broadcast_to(x[:, None, :], rows)

    def by_group(x):
        return jnp.broadcast_to(x[:, None, :], (groups, shards // groups, width)).reshape(shards, width)

    place = iota(rows, 1)
    high = by_group((wanted[...] >> 8).astype(F32))
    low = by_group((wanted[...] & 255).astype(F32))
    tail = jnp.where(place == 0, spread(ids), jnp.where(place == 1, spread(high), spread(low)))
    buf[:, slots : slots + 8, :] = tail.astype(BF16)
    for read, write in zip(features, writes):
        read.wait()
        write.start()
    for write in writes:
        write.wait()


def field_events(tail):
    blocks = tail.shape[0]
    row = tail[...].astype(F32)[:, 0:1, :]
    shape = (blocks * 16, 128)
    spread = jnp.broadcast_to(row, (blocks, 16, 128)).reshape(shape)
    return jnp.where((iota(shape, 1) & 15) == (iota(shape, 0) & 15), spread, 0.0).astype(BF16)


def columns_of(masked, field):
    lane = iota((128, 256), 0) >> 4
    part = iota((128, 256), 1) >> 7
    weight = jnp.where(lane == 2 * field + part, 1.0, 0.0).astype(BF16)
    both = dot(masked, weight).astype(BF16)
    return both[:, :128], both[:, 128:]


def rows_of(masked, fields):
    shape = (16 * fields, 128)
    weight = jnp.where(iota(shape, 1) >> 4 == iota(shape, 0) >> 3, 1.0, 0.0).astype(BF16)
    return dot_nt(weight, masked).astype(BF16)


def one_hot_columns(high, low, count):
    rows = low.shape[0]
    one, zero, none = (jnp.full((rows, 128), x, BF16) for x in (1.0, 0.0, -1.0))
    lanes = [(iota((rows, 128), 1) + 128 * t).astype(F32).astype(BF16) for t in range(2)]
    pieces = []
    for block in range(count // 256):
        key = jnp.where(high == jnp.full((rows, 128), block, BF16), low, none)
        pieces += [jnp.where(lane == key, one, zero) for lane in lanes]
    return jnp.concatenate(pieces, axis=1)


def one_hot_rows(high, low, count, start=0):
    events = low.shape[1]
    shape = (256, events)
    one, zero = jnp.full(shape, 1.0, BF16), jnp.full(shape, 0.0, BF16)
    place = iota(shape, 0).astype(F32).astype(BF16)
    pieces = []
    for block in range(count // 256):
        number = jnp.asarray(start + block, jnp.int32).astype(F32).astype(BF16)
        key = jnp.where(high == jnp.full((1, events), number, BF16), low, jnp.full((1, events), -1.0, BF16))
        pieces.append(jnp.where(place == jnp.broadcast_to(key, shape), one, zero))
    return jnp.concatenate(pieces, axis=0)


def wanted_values(tail):
    rows = tail[...].astype(F32)[:, 0]
    return rows[:, 1], rows[:, 2]


def fetch_kernel(place, tail, memory, out, wanted):
    high, low = wanted_values(tail)
    wanted[...] = jnp.concatenate([high, low], axis=0).astype(BF16)
    groups = high.shape[0]
    shape = (groups * 128, 128)
    here = iota(shape, 1) == (iota(shape, 0) & 127)

    def spread(x):
        wide = jnp.broadcast_to(x[:, None, :], (groups, 128, 128)).reshape(shape)
        return jnp.where(here, wide, 0.0).astype(BF16)

    ones = jnp.full((128, 128), 1.0, BF16)
    high, low = (dot(spread(x), ones).astype(BF16) for x in (high, low))
    selector = one_hot_columns(high, low, memory.shape[0])
    out[...] = dot(selector, memory[...]).astype(BF16)


def cosine(x):
    turns = jnp.floor(x * (0.5 / math.pi) + 0.5)
    rest = x * 0.5 - turns * PI_HIGH
    rest = rest - turns * PI_LOW
    square = rest * rest
    series = jnp.full_like(x, 1.0 / math.factorial(13))
    for power in (11, 9, 7, 5, 3, 1):
        series = series * square + (-1.0) ** (power // 2) / math.factorial(power)
    sine = series * rest
    return 1.0 - 2.0 * (sine * sine)


def source_kernel(tail, memory, freq, current, timing, rows, cols):
    masked = field_events(tail)
    group = iota((128, 128), 0) >> 4
    weight = jnp.where(group == iota((128, 128), 1) + 2, 1.0, 0.0).astype(BF16)
    cols[...] = dot(masked, weight).astype(BF16)
    rows[...] = rows_of(masked, rows.shape[0] // 16)
    selector = one_hot_columns(*columns_of(masked, 0), memory.shape[0])
    current[...] = dot(selector, memory[...]).astype(BF16)
    high, low = columns_of(masked, 3)
    timing[...] = cosine((high.astype(F32) * 256.0 + low.astype(F32)) * freq[...]).astype(BF16)


def step_kernel(
    parts,
    message,
    table,
    cols,
    rows,
    bias,
    timing_hbm,
    current_hbm,
    w_input_hbm,
    w_state_hbm,
    w_pair_hbm,
    table_grad,
    grad_high_hbm,
    grad_low_hbm,
    acc,
    acc_neg,
    timing,
    current_ref,
    w_input,
    w_state,
    w_pair,
    grad_high,
    grad_low,
    sems,
):
    table_rows, width = table.shape
    blocks = message.shape[0] // parts
    events = blocks * 16
    factor = 1.0 / width**0.5
    reads = [
        pltpu.make_async_copy(a, b, sems.at[i])
        for i, (a, b) in enumerate(
            ((w_input_hbm, w_input), (w_state_hbm, w_state), (w_pair_hbm, w_pair), (current_hbm, current_ref), (timing_hbm, timing))
        )
    ]
    writes = [
        pltpu.make_async_copy(a, b, sems.at[len(reads) + i])
        for i, (a, b) in enumerate(((grad_high, grad_high_hbm), (grad_low, grad_low_hbm)))
    ]
    for copy in reads:
        copy.start()

    def rows_for(part):
        mine = message[part * blocks : (part + 1) * blocks]
        ids = cols[pl.ds(part * events, events), :].astype(F32)
        spread = [jnp.broadcast_to(ids[:, i : i + 1], ids.shape).astype(BF16) for i in range(4)]
        partner = dot(one_hot_columns(spread[0], spread[1], table_rows), table[...]).astype(BF16)
        negative = dot(one_hot_columns(spread[2], spread[3], table_rows), table[...]).astype(BF16)
        return mine[:, 0:16, :].reshape(events, 128), partner, negative

    first_rows = [rows_for(part) for part in range(AHEAD)]
    for copy in reads:
        copy.wait()
    w_in, w_rec, pair = w_input[...], w_state[...], w_pair[...]
    w_gates = jnp.concatenate([w_in[:, : 2 * width], w_rec[:, : 2 * width]], axis=0)
    w_back = jnp.concatenate([w_in[:width, :], pair], axis=1)
    gate = bias[...].reshape(1, -1)

    def one_part(part):
        span = pl.ds(part * events, events)
        feature, partner, negative = first_rows[part] if part < AHEAD else rows_for(part)
        current = current_ref[span, :]
        joined = jnp.concatenate([partner, feature, timing[span, :]], axis=1)
        gates = dot(jnp.concatenate([joined, current], axis=1), w_gates) + gate[:, : 2 * width]
        reset = jax.nn.sigmoid(gates[:, :width])
        update = jax.nn.sigmoid(gates[:, width:])
        recurrent = dot(current, w_rec[:, 2 * width :])
        candidate = jnp.tanh(dot(joined, w_in[:, 2 * width :]) + gate[:, 2 * width :] + reset * recurrent)
        change = current.astype(F32) - candidate
        renewed = candidate + update * change
        key_pos = dot(partner, pair)
        key_neg = dot(negative, pair)
        score_pos = jnp.sum(renewed * key_pos, axis=1, keepdims=True) * factor
        score_neg = jnp.sum(renewed * key_neg, axis=1, keepdims=True) * factor
        weight_pos = jax.nn.sigmoid(-score_pos) * -factor
        weight_neg = jax.nn.sigmoid(score_neg) * factor
        grad_renewed = weight_pos * key_pos + weight_neg * key_neg
        grad_keypos = (weight_pos * renewed).astype(BF16)
        grad_keyneg = (weight_neg * renewed).astype(BF16)
        through = grad_renewed * update
        grad_cand = (grad_renewed - through) * (1.0 - candidate * candidate)
        gated = grad_cand * reset
        grad_reset = (gated * recurrent * (1.0 - reset)).astype(BF16)
        grad_update = (through * change * (1.0 - update)).astype(BF16)
        input_back = jnp.concatenate([grad_reset, grad_update, grad_cand.astype(BF16), grad_keypos], axis=1)
        state_back = jnp.concatenate([grad_reset, grad_update, gated.astype(BF16)], axis=1)
        high, low = split(through + dot_nt(state_back, w_rec))
        grad_high[span, :] = high
        grad_low[span, :] = low
        high, low = split(dot_nt(input_back, w_back))
        return high, low, grad_keyneg

    done = [one_part(part) for part in range(parts)]
    grads = jnp.concatenate([x[0] for x in done] + [x[1] for x in done], axis=0)
    grads_neg = jnp.concatenate([x[2] for x in done], axis=0)
    for first in range(table_rows // 256):
        span = pl.ds(first * 256, 256)
        left = one_hot_rows(rows[16:17, :], rows[24:25, :], 256, first)
        acc[span, :] = dot(jnp.concatenate([left, left], axis=1), grads)
        acc_neg[span, :] = dot(one_hot_rows(rows[32:33, :], rows[40:41, :], 256, first), grads_neg)
    for copy in writes:
        copy.start()
    high, low = split(acc_neg[...])
    both = jnp.concatenate([high, low], axis=1)
    total = acc[...] + dot_nt(both, jnp.concatenate([pair, pair], axis=1))
    table_grad[...] = total.astype(BF16)
    for copy in writes:
        copy.wait()


def hold_kernel(source, out):
    out[...] = source[...]


def source_scatter_kernel(rows, grad_high, grad_low, out):
    count = out.shape[0]
    selector = one_hot_rows(rows[0:1, :], rows[8:9, :], count, pl.program_id(0) * (count // 256))
    out[...] = dot(jnp.concatenate([selector] * 2, axis=1), jnp.concatenate([grad_high[...], grad_low[...]], axis=0))


def returned_kernel(wanted, returned, state_grad, out):
    groups = wanted.shape[0] // 2
    high, low = wanted[0:groups, :], wanted[groups:, :]
    count = out.shape[0]
    start = pl.program_id(0) * (count // 256)
    pieces = [one_hot_rows(high[g : g + 1, :], low[g : g + 1, :], count, start) for g in range(high.shape[0])]
    selector = jnp.concatenate(pieces, axis=1)
    out[...] = (state_grad[...] + dot(selector, returned[...])).astype(BF16)


def step_call(message, table, cols, rows, gate_bias, timing, current, w_input, w_state, w_pair):
    table_rows, width = table.shape
    events = current.shape[0]
    in_place = pl.BlockSpec(memory_space=pltpu.HBM)
    return call(
        functools.partial(step_kernel, STEP_PARTS),
        (
            jax.ShapeDtypeStruct((table_rows, width), BF16),
            pltpu.HBM((events, width), BF16),
            pltpu.HBM((events, width), BF16),
        ),
        (message, table, cols, rows, gate_bias, timing, current, w_input, w_state, w_pair),
        in_specs=[whole(x.shape) for x in (message, table, cols, rows, gate_bias)] + [in_place] * 5,
        out_specs=(whole((table_rows, width)), in_place, in_place),
        scratch=[
            pltpu.VMEM((table_rows, width), F32),
            pltpu.VMEM((table_rows, width), F32),
            pltpu.VMEM(timing.shape, BF16),
            pltpu.VMEM((events, width), BF16),
            pltpu.VMEM(w_input.shape, BF16),
            pltpu.VMEM(w_state.shape, BF16),
            pltpu.VMEM(w_pair.shape, BF16),
            pltpu.VMEM((events, width), BF16),
            pltpu.VMEM((events, width), BF16),
            pltpu.SemaphoreType.DMA((7,)),
        ],
        flops=2 * events * width * (5 * table_rows + 3 * 4 * width + 3 * 3 * width),
        moved=8 * events * width,
        trans=events * width * 3,
        name="step",
    )


def local(
    memory,
    event_feat,
    event_source,
    event_partner,
    event_negative,
    event_time,
    event_count,
    requests,
    w_input,
    w_state,
    w_pair,
    gate_bias,
    time_freq,
):
    nodes = lax.axis_size("node")
    peers = lax.axis_size("event")
    shards = nodes * peers
    group_rows, width = memory.shape
    _, groups, per_group = requests.shape
    table_rows = groups * per_group
    slots, feat_width = event_feat.shape[2:]
    events = shards * slots

    w_input, w_state, w_pair, gate_bias, time_freq, memory = map(in_hbm, (w_input, w_state, w_pair, gate_bias, time_freq.reshape(1, -1), memory))
    flat = [x[0].T for x in (event_source, event_partner, event_negative, event_time)]
    args = tuple(map(in_hbm, (event_feat[0], *flat, event_count, requests[0])))
    in_place = pl.BlockSpec(memory_space=pltpu.HBM)
    message = call(
        functools.partial(pack_kernel, group_rows, table_rows),
        pltpu.HBM((shards, slots + 8, feat_width), BF16),
        args,
        in_specs=[in_place] * len(args),
        out_specs=in_place,
        scratch=[
            pltpu.VMEM((shards, slots + 8, feat_width), BF16),
            *(pltpu.VMEM(x.shape, x.dtype) for x in args[1:]),
            pltpu.SemaphoreType.DMA((len(args) - 1 + 2 * PACK_CHUNKS,)),
        ],
        moved=2 * events * feat_width * 2,
        name="pack",
    )
    held = call(
        hold_kernel,
        pltpu.VMEM(memory.shape, BF16),
        (memory,),
        in_specs=[whole(memory.shape)],
        out_specs=whole(memory.shape),
        moved=8 * group_rows * width,
        name="hold",
    )
    message = lax.all_to_all(message, ("node", "event"), 0, 0, tiled=True)
    place = lax.axis_index("event").astype(jnp.int32).reshape(1)
    by_peer = message.reshape(nodes, peers, slots + 8, feat_width)
    tail_spec = pl.BlockSpec((nodes, 1, 8, feat_width), lambda i, at: (0, at[0], slots // 8, 0))
    fetched, wanted = call(
        fetch_kernel,
        (jax.ShapeDtypeStruct((table_rows, width), BF16), jax.ShapeDtypeStruct((2 * groups, per_group), BF16)),
        (place, by_peer, held),
        in_specs=[tail_spec, whole(memory.shape)],
        out_specs=(whole((table_rows, width)), whole((2 * groups, per_group))),
        flops=2 * table_rows * group_rows * width,
        moved=group_rows * width * 2,
        name="fetch",
        prefetch=1,
    )
    table = lax.all_to_all(fetched.reshape(groups, per_group, width), "node", 0, 0, tiled=True).reshape(table_rows, width)

    block = 1024
    turns = events // block
    rows_block = lambda i: (i, 0)
    current, timing, rows, cols = call(
        source_kernel,
        (
            pltpu.HBM((events, width), BF16),
            pltpu.HBM((events, feat_width), BF16),
            jax.ShapeDtypeStruct((48, events), BF16),
            jax.ShapeDtypeStruct((events, feat_width), BF16),
        ),
        (message, held, time_freq),
        grid=(turns,),
        in_specs=[
            pl.BlockSpec((block // slots, 8, feat_width), lambda i: (i, slots // 8, 0)),
            whole(memory.shape),
            whole((1, feat_width)),
        ],
        out_specs=(
            pl.BlockSpec((block, width), rows_block),
            pl.BlockSpec((block, feat_width), rows_block),
            pl.BlockSpec((48, block), lambda i: (0, i)),
            pl.BlockSpec((block, feat_width), rows_block),
        ),
        flops=2 * events * group_rows * width,
        moved=4 * events * width,
        trans=events * feat_width,
        name="source",
    )
    table_grad, grad_high, grad_low = step_call(
        message, table, cols, rows, gate_bias, in_hbm(timing), in_hbm(current), w_input, w_state, w_pair
    )
    returned = lax.all_to_all(table_grad.reshape(groups, per_group, width), "node", 0, 0, tiled=True).reshape(table_rows, width)
    node_block = 1024
    state_grad = call(
        source_scatter_kernel,
        jax.ShapeDtypeStruct((group_rows, width), F32),
        (rows, in_hbm(grad_high), in_hbm(grad_low)),
        grid=(group_rows // node_block,),
        in_specs=[whole((16, events)), whole(grad_high.shape), whole(grad_low.shape)],
        out_specs=pl.BlockSpec((node_block, width), rows_block),
        flops=4 * events * group_rows * width,
        moved=8 * events * width,
        name="scatter",
    )
    node_block = 1024
    total = call(
        returned_kernel,
        jax.ShapeDtypeStruct((group_rows, width), BF16),
        (wanted, returned, state_grad),
        grid=(group_rows // node_block,),
        in_specs=[whole(wanted.shape), whole((table_rows, width)), pl.BlockSpec((node_block, width), rows_block)],
        out_specs=pl.BlockSpec((node_block, width), rows_block),
        flops=2 * table_rows * group_rows * width,
        moved=6 * group_rows * width,
        name="returned",
    )
    shares = lax.all_to_all(total.reshape(peers, group_rows // peers, width), "event", 0, 0, tiled=True)
    return jnp.sum(shares.astype(F32), axis=0)


def solution(mesh):
    in_specs = (
        P("node", None),
        P(("node", "event"), None, None, None),
        P(("node", "event"), None, None),
        P(("node", "event"), None, None),
        P(("node", "event"), None, None),
        P(("node", "event"), None, None),
        P(("node", "event"), None),
        P(("node", "event"), None, None),
        P(),
        P(),
        P(),
        P(),
        P(),
    )
    out_specs = P(("node", "event"), None)
    return jax.shard_map(local, mesh=mesh, in_specs=in_specs, out_specs=out_specs, check_vma=False)
```
